512 devices in a mesh: group: 2 (over z_hi), dev: 256 (over x, z_lo, y, core).
Axes of the slice: x: 4, y: 4, z: 16 (z_hi: 2, z_lo: 8; z = z_hi * 8 + z_lo), core: 2. Of those that a mesh axis runs over, the one named last changes fastest.
Arguments:
- teacher: bfloat16 [3072, 8192], P(('group', 'dev')), may hold values from -6 to 6
- owner: int32 [2, 256], replicated, may hold values from 0 to 255, each once within a row
- proj_tiles: bfloat16 [131072, 256], P('dev'), may hold values from -0.0625 to 0.0625
- student_tiles: bfloat16 [49152, 256], P(('group', 'dev')), may hold values from -6 to 6
Outputs:
- grad_proj_tiles: bfloat16 [131072, 256], P('dev')
- grad_student_tiles: bfloat16 [49152, 256], P(('group', 'dev'))
The draws below stay inside these ranges and needn't reach their ends.
Inputs may be any that keep to these rules, and one draw needn't show every extreme that they name: Each row of owner is a permutation of 0 to 255.
All inputs are finite; a program needn't handle non-finite values.
Results may differ from the reference program's by a relative error of at most 0.0069.
Values may be sent and summed in bfloat16 or wider, within the bound.
A program may use at most 64 MiB of HBM per device.

```python
import math
import jax
import jax.numpy as jnp
from jax import lax

DT = 8192
DS = 4096
TOK_DEV = 6
FEAT_SPLIT = 16
BT = 512
BS = 256
SPAN = 96
TOKENS = 3072
N_GROUP = 2
N_DEV = 256


def block_scale(stream_key, dims, split, smallest, largest):
    def one(position, shards_of):
        heights = jax.random.uniform(jax.random.fold_in(jax.random.fold_in(stream_key, 6), position), (shards_of,), jnp.float32, smallest / len(split), largest / len(split))
        return jnp.repeat(jnp.exp(heights), dims[position] // shards_of).reshape((-1,) + (1,) * (len(dims) - position - 1))

    loudness = one(*split[0])
    for cut in split[1:]:
        loudness = loudness * one(*cut)
    return loudness


def scatter_about(own_key, shape, width, limit, cuts=(), kind=jnp.bfloat16):
    array = jax.random.normal(own_key, shape, jnp.float32) * width
    if len(cuts) > 0:
        array = block_scale(own_key, shape, cuts, -0.22, 0.18) * array
    return jnp.clip(array, min=-limit, max=limit).astype(kind)


def setup_inputs(seed: int = 0) -> dict:
    splits = jax.random.split(jax.random.key(seed), 5)
    return {
        "teacher": scatter_about(splits[0], (TOKENS, DT), 1.0, 6.0, ((0, 512),)),
        "owner": jax.vmap(lambda own: jax.random.permutation(own, N_DEV))(jax.random.split(splits[1], N_GROUP)).reshape((N_GROUP, N_DEV)).astype(jnp.int32),
        "proj_tiles": scatter_about(splits[2], (N_DEV * BT, BS), DT ** -0.5, 0.0625, ((0, 256),)),
        "student_tiles": scatter_about(splits[3], (N_GROUP * N_DEV * SPAN, BS), 1.0, 6.0, ((0, 512),)),
    }


epsilon = 1e-06

def reference(teacher, owner, proj_tiles, student_tiles):
    spread = N_DEV // FEAT_SPLIT
    block_teacher = DT // FEAT_SPLIT
    block_student = DS // spread
    half_rows = N_DEV * TOK_DEV
    span_rows = half_rows // FEAT_SPLIT
    weight = proj_tiles.reshape(spread, FEAT_SPLIT, block_teacher, block_student).transpose(1, 2, 0, 3).reshape(DT, DS)
    student = student_tiles.reshape(N_GROUP, spread, FEAT_SPLIT, span_rows, block_student).transpose(0, 2, 3, 1, 4).reshape(N_GROUP, half_rows, DS)
    states = teacher.reshape(N_GROUP, half_rows, DT)
    grad_weight = jnp.zeros((DT, DS), jnp.float32)
    grad_list = []
    for half_index in range(N_GROUP):
        projected = jnp.dot(states[half_index], weight, preferred_element_type=jnp.float32)
        owner_row = owner[half_index].astype(jnp.int32)
        ordered = jnp.take(projected.reshape(N_DEV, TOK_DEV, DS), owner_row, axis=0).reshape(half_rows, DS)
        root_mean = jnp.sqrt(lax.optimization_barrier(jnp.mean(ordered * ordered, axis=1, keepdims=True)) + epsilon)
        normed = ordered / root_mean
        target = student[half_index].astype(jnp.float32)
        grad_list.append((target - normed).astype(jnp.bfloat16))
        upstream = normed - target
        inner_mean = lax.optimization_barrier(jnp.mean(upstream * normed, axis=1, keepdims=True))
        row_slope = ((upstream - normed * inner_mean) / root_mean).astype(jnp.bfloat16)
        teacher_order = jnp.zeros((N_DEV, TOK_DEV, DS), jnp.bfloat16).at[owner_row].set(row_slope.reshape(N_DEV, TOK_DEV, DS))
        grad_weight = grad_weight + lax.dot_general(states[half_index], teacher_order.reshape(half_rows, DS), (((0,), (0,)), ((), ())), preferred_element_type=jnp.float32)
    scale_factor = 1.0 / math.sqrt(N_GROUP * half_rows)
    grad_proj = (grad_weight * scale_factor).astype(jnp.bfloat16)
    grad_proj = grad_proj.reshape(FEAT_SPLIT, block_teacher, spread, block_student).transpose(2, 0, 1, 3).reshape(N_DEV * block_teacher, block_student)
    grad_student = jnp.stack(grad_list).reshape(N_GROUP, FEAT_SPLIT, span_rows, spread, block_student).transpose(0, 3, 1, 2, 4).reshape(N_GROUP * N_DEV * span_rows, block_student)
    return (grad_proj, grad_student)
```

```python
import functools
import math

import jax
import jax.numpy as jnp
from jax import lax
from jax.experimental import pallas as pl
from jax.experimental.pallas import tpu as pltpu
from jax.sharding import PartitionSpec as P

MESH = pl.DeviceIdType.MESH
DS = 4096
EPS = 1e-06
HIGH = lax.Precision.HIGHEST
ROWS = 6
BLOCK = 96
BT = 512
BS = 256


def flip(v, m):
    if m == 0:
        return v
    if m == 1:
        return v + 1 - 2 * (v % 2)
    if m == 2:
        return v + 2 - 4 * (v // 2)
    return 3 - v


def flip1(v, m):
    return 1 - v if m else v


def remote(src, dst, ss, rs, dev):
    return pltpu.make_async_remote_copy(
        src_ref=src, dst_ref=dst, send_sem=ss, recv_sem=rs, device_id=dev, device_id_type=MESH
    )


def kernel(
    teacher, owner, proj, student,
    gproj, gstud,
    arecv, xa, xg, y3, x3, ycs, ycr, yown, cs, cr, pbuf, es, er, dall, xs, xt, gs, gr, gacc,
    a_s, a_r, z_s, z_r, xp_s, xp_r, xm_s, xm_r, hp_s, hp_r, hm_s, hm_r,
    co_s, co_r, c_s, c_r, e_s, e_r, d_s, d_r, dc_s, dc_r, g_s, g_r, far,
):
    g = lax.axis_index("group")
    d = lax.axis_index("dev")
    x, zl, y, c = d // 64, (d // 8) % 8, (d // 2) % 4, d % 2
    zk, z0 = zl // 2, zl % 2
    zz = g * 8 + zl

    def dev(x=x, zk=zk, z0=z0, y=y, c=c):
        return (g, ((x * 8 + zk * 2 + z0) * 4 + y) * 2 + c)

    def zdev(step):
        to = (zz + step) % 16
        return (to // 8, ((x * 8 + to % 8) * 4 + y) * 2 + c)

    f = z0 * 8 + y * 2 + c
    chips = [(a, b) for a in range(2) for b in range(4) if (a, b) != (0, 0)]
    fpeers = [(a, b, e) for a in range(2) for b in range(4) for e in range(2) if (a, b, e) != (0, 0, 0)]

    def fdev(a, b, e):
        return dev(z0=flip1(z0, a), y=flip(y, b), c=flip1(c, e))

    def findex(a, b, e):
        return flip1(z0, a) * 8 + flip(y, b) * 2 + flip1(c, e)

    xup, xdown = dev(x=(x + 1) % 4), dev(x=(x + 3) % 4)
    zup, zdown = dev(zk=(zk + 1) % 4), dev(zk=(zk + 3) % 4)
    mate = dev(c=1 - c)
    has_up, has_down = zk < 3, zk > 0

    bar = pltpu.get_barrier_semaphore()

    def greet(to):
        pl.semaphore_signal(bar, inc=1, device_id=to, device_id_type=MESH)

    greet(zdev(4))
    greet(zdev(12))
    for a, b, e in fpeers:
        greet(fdev(a, b, e))
    greet(xup)
    greet(xdown)

    @pl.when(has_up)
    def _():
        greet(zup)

    @pl.when(has_down)
    def _():
        greet(zdown)

    near = jnp.where(has_up, 1, 0) + jnp.where(has_down, 1, 0)
    pl.semaphore_wait(bar, 19 + near)
    pl.semaphore_signal(far, inc=1, device_id=zdev(4), device_id_type=MESH)

    acopies = []
    for n, (a, b, e) in enumerate(fpeers):
        to = findex(a, b, e)
        cp = remote(
            teacher.at[:, pl.ds(pl.multiple_of(to * BT, BT), BT)], arecv.at[f], a_s.at[n], a_r.at[n], fdev(a, b, e)
        )
        cp.start()
        acopies.append(cp)
    arecv[f] = teacher[:, pl.ds(pl.multiple_of(f * BT, BT), BT)]
    for cp in acopies:
        cp.wait_recv()
    for n in range(16):
        xa[n * ROWS : (n + 1) * ROWS, :] = arecv[n].astype(jnp.float32)
    own = xg.at[zk, x]
    xg[zk, x] = xa[...].astype(jnp.bfloat16)

    def zcopy(k, to):
        return remote(xg.at[k, x], xg.at[k, x], z_s.at[k], z_r.at[k], to)

    def zcopy2(k, to):
        return remote(xg.at[k, x], xg.at[k, x], z_s.at[4 + k], z_r.at[k], to)

    def xpcopy(k, at):
        return remote(xg.at[k, at], xg.at[k, at], xp_s.at[k], xp_r.at[k], xup)

    def xmcopy(k, at):
        return remote(xg.at[k, at], xg.at[k, at], xm_s.at[k], xm_r.at[k], xdown)

    half = BLOCK // 2
    lo, hi = pl.ds(0, half), pl.ds(half, half)
    left, right, opposite = (x + 3) % 4, (x + 1) % 4, (x + 2) % 4

    def hpcopy(k, at):
        return remote(xg.at[k, at, lo], xg.at[k, at, lo], hp_s.at[k], hp_r.at[k], xup)

    def hmcopy(k, at):
        return remote(xg.at[k, at, hi], xg.at[k, at, hi], hm_s.at[k], hm_r.at[k], xdown)

    def xsend(k):
        xpcopy(k, x).start()
        xmcopy(k, x).start()

    def xforward(k):
        xpcopy(k, left).wait_recv()
        hpcopy(k, left).start()
        xmcopy(k, right).wait_recv()
        hmcopy(k, right).start()

    def multiply(k):
        hpcopy(k, opposite).wait_recv()
        hmcopy(k, opposite).wait_recv()
        part = jnp.dot(
            xg[k].reshape(4 * BLOCK, BT), proj[...], preferred_element_type=jnp.float32
        )
        for i in range(4):
            for n in range(16):
                r = (i * 16 + n) * ROWS
                y3[(i * 4 + k) * 16 + n, 0:ROWS, :] = part[r : r + ROWS, :]

    k1 = jnp.where(zk == 0, 1, zk - 1)
    k2 = jnp.where(zk == 0, 2, jnp.where(zk == 1, 2, jnp.where(zk == 2, 3, 1)))
    k3 = jnp.where(zk < 2, 3, 0)
    order = [zk, k1, k2, k3]

    @pl.when(has_up)
    def _():
        zcopy(zk, zup).start()

    @pl.when(has_down)
    def _():
        zcopy2(zk, zdown).start()

    xsend(zk)
    for i in range(1, 6):
        if i <= 4:
            xforward(order[i - 1])
        if i <= 3:
            k = order[i]
            zcopy(k, zup).wait_recv()

            @pl.when((k < zk) & has_up)
            def _():
                zcopy(k, zup).start()

            @pl.when((k > zk) & has_down)
            def _():
                zcopy(k, zdown).start()

            xsend(k)
        if i >= 2:
            multiply(order[i - 2])

    def build(fi):
        return [y3[owner[g, fi * 16 + n]] for n in range(16)]

    def cocopy(j):
        return remote(ycs.at[j], ycr.at[j], co_s.at[j], co_r.at[j], mate)

    allchips = [(0, 0)] + chips
    order_c = chips + [(0, 0)]
    for a, b in order_c:
        j = a * 4 + b
        theirs = build(findex(a, b, 1))
        for n in range(16):
            pbuf[n * ROWS : (n + 1) * ROWS, :] = theirs[n][0:ROWS]
        ycs[j] = pbuf[...].astype(jnp.bfloat16)
        cocopy(j).start()
        mine = build(findex(a, b, 0))
        for n in range(16):
            yown[j, n * ROWS : (n + 1) * ROWS, :] = mine[n][0:ROWS]

    def ccopy(a, b):
        j = a * 4 + b
        return remote(cs.at[j], cr.at[j], c_s.at[j], c_r.at[j], fdev(a, b, 0))

    for a, b in order_c:
        j = a * 4 + b
        cocopy(j).wait_recv()
        total = yown[j] + ycr[j].astype(jnp.float32)
        if j:
            cs[j] = total.astype(jnp.bfloat16)
            ccopy(a, b).start()
        else:
            pbuf[...] = total

    @pl.loop(0, 4)
    def _(k):
        for i in range(4):
            block = xg[k, i].astype(jnp.float32)
            for n in range(16):
                x3[(i * 4 + k) * 16 + n, 0:ROWS, :] = block[n * ROWS : (n + 1) * ROWS, :]

    total = pbuf[...]
    for a, b in chips:
        ccopy(a, b).wait_recv()
        total = total + cr[a * 4 + b].astype(jnp.float32)
    pbuf[...] = total

    target = student[...].astype(jnp.float32)
    ones = jnp.ones((8, BS), jnp.float32)
    dims = (((1,), (1,)), ((), ()))
    sq = lax.dot_general(ones, total * total, dims, precision=HIGH, preferred_element_type=jnp.float32)
    sp = lax.dot_general(ones, total * target, dims, precision=HIGH, preferred_element_type=jnp.float32)
    which = lax.broadcasted_iota(jnp.int32, (8, BLOCK), 0)
    es[...] = jnp.zeros((8, 128), jnp.float32)
    es[:, 0:BLOCK] = jnp.where(which == 0, sq, sp)
    qpeers = [(a, b) for a in range(4) for b in range(4) if (a, b) != (0, 0)]
    ecopies = []
    for a, b in qpeers:
        n = a * 4 + b
        cp = remote(es, er.at[n], e_s.at[n], e_r.at[n], dev(x=flip(x, a), zk=flip(zk, b)))
        cp.start()
        ecopies.append(cp)

    @pl.loop(0, 16)
    def _(fi):
        for n in range(16):
            xs[fi, n * ROWS : (n + 1) * ROWS, :] = x3[owner[g, fi * 16 + n]][0:ROWS]

    for n in range(12):
        lo_f, row = divmod(n * 128, BLOCK)
        rows = []
        need = 128
        while need:
            take = min(BLOCK - row, need)
            rows.append(xs[lo_f, row : row + take, :])
            need -= take
            lo_f, row = lo_f + 1, 0
        xt[:, n * 128 : (n + 1) * 128] = jnp.concatenate(rows, axis=0).T.astype(jnp.bfloat16)

    sums = es[...]
    for cp, (a, b) in zip(ecopies, qpeers):
        cp.wait_recv()
        sums = sums + er[a * 4 + b]
    sums = sums[:, 0:BLOCK]
    row = lax.broadcasted_iota(jnp.int32, (8, BS), 0)
    cols = (((0,), (0,)), ((), ()))
    sq = lax.dot_general(
        sums, jnp.where(row == 0, 1.0, 0.0), cols, precision=HIGH, preferred_element_type=jnp.float32
    )
    sp = lax.dot_general(
        sums, jnp.where(row == 1, 1.0, 0.0), cols, precision=HIGH, preferred_element_type=jnp.float32
    )
    total = pbuf[...]
    root = jnp.sqrt(sq / DS + EPS)
    normed = total / root
    inner = (sq / (root * root) - sp / root) / DS
    upstream = normed - target
    slope = ((upstream - normed * inner) / root).astype(jnp.bfloat16)
    gstud[...] = (target - normed).astype(jnp.bfloat16)
    dall[f] = slope

    def dcopy(n, a, b):
        return remote(dall.at[f], dall.at[f], d_s.at[n], d_r.at[n], fdev(a, b, 0))

    def dccopy(n, at):
        return remote(dall.at[at], dall.at[at], dc_s.at[n], dc_r.at[n], mate)

    for a, b in chips:
        dcopy(a * 4 + b, a, b).start()
    dccopy(0, f).start()
    for a, b in chips:
        n = a * 4 + b
        at = findex(a, b, 0)
        remote(dall.at[at], dall.at[at], d_s.at[n], d_r.at[n], mate).wait_recv()
        dccopy(n, at).start()
    for a, b in allchips:
        dccopy(a * 4 + b, findex(a, b, 1)).wait_recv()

    part = jnp.dot(xt[...], dall[...].reshape(16 * BLOCK, BS), preferred_element_type=jnp.float32)
    gacc[...] = part
    gs[...] = part.astype(jnp.bfloat16)
    pl.semaphore_wait(far, 1)
    gcopy = remote(gs, gr, g_s, g_r, zdev(8))
    gcopy.start()
    for cp in acopies + ecopies:
        cp.wait_send()

    @pl.when(has_up)
    def _():
        zcopy(zk, zup).wait_send()

    @pl.when(has_down)
    def _():
        zcopy2(zk, zdown).wait_send()

    for k in order[1:]:

        @pl.when(((k < zk) & has_up) | ((k > zk) & has_down))
        def _():
            zcopy(k, zup).wait_send()

    for k in range(4):
        xpcopy(k, x).wait_send()
        xmcopy(k, x).wait_send()
        hpcopy(k, left).wait_send()
        hmcopy(k, right).wait_send()
    for a, b in allchips:
        n = a * 4 + b
        cocopy(n).wait_send()
        dccopy(n, f).wait_send()
        if n:
            ccopy(a, b).wait_send()
            dcopy(n, a, b).wait_send()
    gcopy.wait_recv()
    gproj[...] = ((gacc[...] + gr[...].astype(jnp.float32)) * (1.0 / math.sqrt(3072))).astype(jnp.bfloat16)
    gcopy.wait_send()


def shards(teacher, owner, proj_tiles, student_tiles):
    bf, f32 = jnp.bfloat16, jnp.float32
    vm, sem = pltpu.VMEM, pltpu.SemaphoreType.DMA
    scratch = [
        vm((16, ROWS, BT), bf), vm((BLOCK, BT), f32), vm((4, 4, BLOCK, BT), bf), vm((256, 8, BS), f32),
        vm((256, 8, BT), f32), vm((8, BLOCK, BS), bf), vm((8, BLOCK, BS), bf), vm((8, BLOCK, BS), f32),
        vm((8, BLOCK, BS), bf), vm((8, BLOCK, BS), bf), vm((BLOCK, BS), f32), vm((8, 128), f32),
        vm((16, 8, 128), f32), vm((16, BLOCK, BS), bf), vm((16, BLOCK, BT), f32), vm((BT, 1536), bf),
        vm((BT, BS), bf), vm((BT, BS), bf), vm((BT, BS), f32),
        sem((16,)), sem((16,)), sem((8,)), sem((4,)), sem((4,)), sem((4,)), sem((4,)), sem((4,)),
        sem((4,)), sem((4,)), sem((4,)), sem((4,)),
        sem((8,)), sem((8,)), sem((8,)), sem((8,)), sem((16,)), sem((16,)), sem((8,)), sem((8,)), sem((8,)), sem((8,)),
        sem, sem, pltpu.SemaphoreType.REGULAR,
    ]
    whole = pl.BlockSpec(memory_space=pltpu.VMEM)
    return pl.pallas_call(
        kernel,
        name="distill",
        out_shape=(jax.ShapeDtypeStruct((BT, BS), bf), jax.ShapeDtypeStruct((BLOCK, BS), bf)),
        in_specs=[whole, pl.BlockSpec(memory_space=pltpu.SMEM), whole, whole],
        out_specs=(whole, whole),
        scratch_shapes=scratch,
        compiler_params=pltpu.CompilerParams(
            collective_id=0, has_side_effects=True, vmem_limit_bytes=48 * 2**20
        ),
    )(teacher, owner, proj_tiles, student_tiles)


def solution(mesh):
    placed = (P(("group", "dev"), None), P(), P("dev", None), P(("group", "dev"), None))
    return jax.shard_map(
        shards,
        mesh=mesh,
        in_specs=placed,
        out_specs=(P("dev", None), P(("group", "dev"), None)),
        check_vma=False,
    )
```

```python
import math

import jax
import jax.numpy as jnp
from jax import lax
from jax.experimental import pallas as pl
from jax.experimental.pallas import tpu as pltpu
from jax.sharding import PartitionSpec as P

MESH = pl.DeviceIdType.MESH
DS = 4096
EPS = 1e-06
HIGH = lax.Precision.HIGHEST
ROWS = 6
BLOCK = 96
HALF = BLOCK // 2
BT = 512
BS = 256
SCALE = 1.0 / math.sqrt(3072)


def flip(v, m):
    if m == 0:
        return v
    if m == 1:
        return v + 1 - 2 * (v % 2)
    if m == 2:
        return v + 2 - 4 * (v // 2)
    return 3 - v


def flip1(v, m):
    return 1 - v if m else v


def remote(src, dst, ss, rs, dev):
    return pltpu.make_async_remote_copy(
        src_ref=src, dst_ref=dst, send_sem=ss, recv_sem=rs, device_id=dev, device_id_type=MESH
    )


def slopes(total, target, sq, sp):
    root = jnp.sqrt(sq / DS + EPS)
    normed = total / root
    inner = (sq / (root * root) - sp / root) / DS
    upstream = normed - target
    return normed, ((upstream - normed * inner) / root).astype(jnp.bfloat16)


def kernel(
    teacher_in, owner_in, proj_in, student_in,
    gproj, gstud,
    teacher, owner, proj, student,
    arecv, xa, xg, y3, x3, xs, xt, ycs, ycr, yown, cs, cr, pbuf, ps, pr, sr, es, er, dall,
    in_s, a_s, a_r, b_sems, co_s, co_r, c_s, c_r, p_s, p_r, s_s, s_r,
    e_s, e_r, d_s, d_r, dc_s, dc_r, far,
):
    g = lax.axis_index("group")
    d = lax.axis_index("dev")
    x, zl, y, c = d // 64, (d // 8) % 8, (d // 2) % 4, d % 2
    zk, z0 = zl // 2, zl % 2
    zz = g * 8 + zl

    def dev(x=x, zk=zk, z0=z0, y=y, c=c, g=g):
        return (g, ((x * 8 + zk * 2 + z0) * 4 + y) * 2 + c)

    def zdev(step):
        to = (zz + step) % 16
        return (to // 8, ((x * 8 + to % 8) * 4 + y) * 2 + c)

    f = z0 * 8 + y * 2 + c
    chips = [(a, b) for a in range(2) for b in range(4) if (a, b) != (0, 0)]
    fpeers = [(a, b, e) for a in range(2) for b in range(4) for e in range(2) if (a, b, e) != (0, 0, 0)]

    def fdev(a, b, e):
        return dev(z0=flip1(z0, a), y=flip(y, b), c=flip1(c, e))

    def findex(a, b, e):
        return flip1(z0, a) * 8 + flip(y, b) * 2 + flip1(c, e)

    xup, xdown = dev(x=(x + 1) % 4), dev(x=(x + 3) % 4)
    zup, zdown = zdev(2), zdev(14)
    here = g * 4 + zk
    mate, cross = dev(c=1 - c), dev(g=1 - g)
    left, right, opposite = (x + 3) % 4, (x + 1) % 4, (x + 2) % 4

    pending = []

    def begin(cp):
        cp.start()
        pending.append(cp.wait_send)
        return cp

    loads = [
        pltpu.make_async_copy(a, b, in_s.at[n])
        for n, (a, b) in enumerate(
            [(teacher_in, teacher), (owner_in, owner), (proj_in, proj), (student_in, student)]
        )
    ]
    for cp in loads:
        cp.start()
    bar = pltpu.get_barrier_semaphore()

    def greet(to):
        pl.semaphore_signal(bar, inc=1, device_id=to, device_id_type=MESH)

    for step in (2, 14, 4, 12):
        greet(zdev(step))
    for a, b, e in fpeers:
        greet(fdev(a, b, e))
    greet(xup)
    greet(xdown)
    loads[0].wait()
    pl.semaphore_wait(bar, 21)
    pl.semaphore_signal(far, inc=1, device_id=zdev(4), device_id_type=MESH)

    acopies = []
    for n, (a, b, e) in enumerate(fpeers):
        to = findex(a, b, e)
        acopies.append(
            begin(
                remote(
                    teacher.at[:, pl.ds(pl.multiple_of(to * BT, BT), BT)], arecv.at[f], a_s.at[n], a_r.at[n], fdev(a, b, e)
                )
            )
        )
    arecv[f] = teacher[:, pl.ds(pl.multiple_of(f * BT, BT), BT)]
    for cp in loads[1:]:
        cp.wait()
    for cp in acopies:
        cp.wait_recv()
    for n in range(16):
        xa[n * ROWS : (n + 1) * ROWS, :] = arecv[n].astype(jnp.float32)
    xg[here, x] = xa[...].astype(jnp.bfloat16)

    zus, zur, zds, zdr, xps, xpr, xms, xmr, xhs, xhr = b_sems

    def view(k, at, h):
        return xg.at[k, at, pl.ds(h * HALF, HALF)]

    def below(s):
        return (here + 8 - s) % 8

    def above(s):
        return (here + s) % 8

    def upcopy(s, h):
        v = view(below(s), x, h)
        return remote(v, v, zus.at[s * 2 + h], zur.at[s * 2 + h], zup)

    def downcopy(s, h):
        v = view(above(s), x, h)
        return remote(v, v, zds.at[s * 2 + h], zdr.at[s * 2 + h], zdown)

    def pcopy(k, at, h):
        v = view(k, at, h)
        return remote(v, v, xps.at[k * 2 + h], xpr.at[k * 2 + h], xup)

    def mcopy(k, at, h):
        v = view(k, at, h)
        return remote(v, v, xms.at[k * 2 + h], xmr.at[k * 2 + h], xdown)

    def hcopy(k, at, h):
        v = view(k, at, h)
        return remote(v, v, xhs.at[k * 2 + h], xhr.at[k * 2 + h], xdown if h else xup)

    def xsend(k):
        for h in range(2):
            begin(pcopy(k, x, h))
            begin(mcopy(k, x, h))

    def xforward(k):
        pcopy(k, left, 0).wait_recv()
        begin(hcopy(k, left, 0))
        mcopy(k, right, 1).wait_recv()
        begin(hcopy(k, right, 1))

    def finish(k):
        pcopy(k, left, 1).wait_recv()
        mcopy(k, right, 0).wait_recv()
        hcopy(k, opposite, 0).wait_recv()
        hcopy(k, opposite, 1).wait_recv()

    def zstep(s):
        for h in range(2):
            if s < 4 or h == 0:
                v = view(below(s), x, h)
                remote(v, v, zus.at[(s - 1) * 2 + h], zur.at[(s - 1) * 2 + h], zup).wait_recv()
                if s < 3 or (s == 3 and h == 0):
                    begin(upcopy(s, h))
            if s < 4 or h == 1:
                v = view(above(s), x, h)
                remote(v, v, zds.at[(s - 1) * 2 + h], zdr.at[(s - 1) * 2 + h], zdown).wait_recv()
                if s < 3 or (s == 3 and h == 1):
                    begin(downcopy(s, h))

    edge = (zk == 0) | (zk == 3)
    first, second = [here], [here]
    for s in range(1, 4):
        up_first = zk + s <= 3
        first.append(jnp.where(up_first, above(s), below(s)))
        second.append(jnp.where(up_first, below(s), above(s)))
    far_block = above(4)
    inner = [here, first[1], jnp.where(edge, first[2], second[1]), jnp.where(edge, first[3], first[2])]
    outer = [jnp.where(edge, second[1], second[2]), jnp.where(edge, second[2], first[3]), second[3], far_block]

    def multiply(k):
        part = jnp.dot(
            xg[k].reshape(4 * BLOCK, BT), proj[...], preferred_element_type=jnp.float32
        )
        for i in range(4):
            for n in range(16):
                r = (i * 16 + n) * ROWS
                y3[(i * 4 + k % 4) * 16 + n, 0:ROWS, :] = part[r : r + ROWS, :]

    def spread(k):
        @pl.loop(0, 4)
        def _(i):
            block = xg[k, i].astype(jnp.float32)
            for n in range(16):
                x3[(i * 4 + k % 4) * 16 + n, 0:ROWS, :] = block[n * ROWS : (n + 1) * ROWS, :]

    def arrange(which, half, first, last):
        @pl.loop(first, last)
        def _(it):
            for j in range(4):
                for n in range(16):
                    r = (j * 16 + n) * ROWS
                    xs[r : r + ROWS, :] = x3[owner[half, (it * 4 + j) * 16 + n]][0:ROWS]
            for m in range(3):
                to = pl.ds(pl.multiple_of(it * 384 + m * 128, 128), 128)
                xt[which, :, to] = xs[m * 128 : (m + 1) * 128, :].T.astype(jnp.bfloat16)

    for h in range(2):
        begin(upcopy(0, h))
        begin(downcopy(0, h))
    xsend(here)
    xforward(here)
    zstep(1)
    xsend(first[1])
    xsend(second[1])
    zstep(2)
    xsend(first[2])
    xforward(first[1])
    xforward(second[1])
    xsend(second[2])
    finish(here)
    multiply(here)
    spread(here)
    zstep(3)
    xsend(first[3])
    xforward(first[2])
    finish(first[1])
    multiply(first[1])
    spread(first[1])
    xforward(first[3])
    xforward(second[2])
    xsend(second[3])
    finish(inner[2])
    multiply(inner[2])
    finish(inner[3])
    multiply(inner[3])

    def build(fi, put):
        for n in range(16):
            put(slice(n * ROWS, (n + 1) * ROWS), y3[owner[g, fi * 16 + n]][0:ROWS])

    def cocopy(j):
        return remote(ycs.at[j], ycr.at[j], co_s.at[j], co_r.at[j], mate)

    allchips = [(0, 0)] + chips
    order_c = chips + [(0, 0)]
    for a, b in order_c:
        j = a * 4 + b

        def put(rows, v):
            pbuf[rows, :] = v

        def keep(rows, v):
            yown[j, rows, :] = v

        build(findex(a, b, 1), put)
        ycs[j] = pbuf[...].astype(jnp.bfloat16)
        begin(cocopy(j))
        build(findex(a, b, 0), keep)

    def ccopy(a, b):
        j = a * 4 + b
        return remote(cs.at[j], cr.at[j], c_s.at[j], c_r.at[j], fdev(a, b, 0))

    for a, b in order_c:
        j = a * 4 + b
        cocopy(j).wait_recv()
        total = yown[j] + ycr[j].astype(jnp.float32)
        if j:
            cs[j] = total.astype(jnp.bfloat16)
            begin(ccopy(a, b))
        else:
            pbuf[...] = total

    pl.semaphore_wait(far, 1)
    scopy = begin(remote(student, sr, s_s, s_r, cross))
    zstep(4)
    xsend(far_block)
    xforward(second[3])
    spread(inner[2])
    spread(inner[3])
    arrange(0, g, 0, 4)
    xforward(far_block)
    for k in outer:
        finish(k)

    total = pbuf[...]
    for a, b in chips:
        ccopy(a, b).wait_recv()
        total = total + cr[a * 4 + b].astype(jnp.float32)
    pbuf[...] = total
    ps[...] = total.astype(jnp.bfloat16)

    target = student[...].astype(jnp.float32)
    ones = jnp.ones((8, BS), jnp.float32)
    dims = (((1,), (1,)), ((), ()))
    sq = lax.dot_general(ones, total * total, dims, precision=HIGH, preferred_element_type=jnp.float32)
    sp = lax.dot_general(ones, total * target, dims, precision=HIGH, preferred_element_type=jnp.float32)
    which = lax.broadcasted_iota(jnp.int32, (2, BLOCK), 0)
    es[...] = jnp.zeros((2, 128), jnp.float32)
    es[:, 0:BLOCK] = jnp.where(which == 0, sq[0:2], sp[0:2])
    ecopies = []
    for side in range(2):
        for a in range(4):
            for b in range(4):
                n = side * 16 + a * 4 + b
                if n:
                    to = dev(x=flip(x, a), zk=flip(zk, b), g=flip1(g, side))
                    ecopies.append((n, begin(remote(es, er.at[n], e_s.at[n], e_r.at[n], to))))
    statecopy = begin(remote(ps, pr, p_s, p_r, cross))

    for k in outer:
        spread(k)
    arrange(1, 1 - g, 0, 4)

    sums = [es[...], jnp.zeros((2, 128), jnp.float32)]
    for n, cp in ecopies:
        cp.wait_recv()
        sums[n // 16] = sums[n // 16] + er[n]
    row = lax.broadcasted_iota(jnp.int32, (2, BS), 0)
    cols = (((0,), (0,)), ((), ()))

    def column(v, n):
        return lax.dot_general(
            v[:, 0:BLOCK], jnp.where(row == n, 1.0, 0.0), cols, precision=HIGH, preferred_element_type=jnp.float32
        )

    normed, slope = slopes(pbuf[...], target, column(sums[0], 0), column(sums[0], 1))
    dall[0, f] = slope
    gstud[...] = (target - normed).astype(jnp.bfloat16)

    def dcopy(s, a, b):
        n = s * 8 + a * 4 + b
        return remote(dall.at[s, f], dall.at[s, f], d_s.at[n], d_r.at[n], fdev(a, b, 0))

    def dccopy(s, n, at):
        return remote(dall.at[s, at], dall.at[s, at], dc_s.at[s * 8 + n], dc_r.at[s * 8 + n], mate)

    def share(s):
        for a, b in chips:
            begin(dcopy(s, a, b))
        begin(dccopy(s, 0, f))

    share(0)
    scopy.wait_recv()
    statecopy.wait_recv()
    _, slope = slopes(
        pr[...].astype(jnp.float32), sr[...].astype(jnp.float32), column(sums[1], 0), column(sums[1], 1)
    )
    dall[1, f] = slope
    share(1)
    for s in range(2):
        for a, b in chips:
            n = a * 4 + b
            at = findex(a, b, 0)
            remote(dall.at[s, at], dall.at[s, at], d_s.at[s * 8 + n], d_r.at[s * 8 + n], mate).wait_recv()
            begin(dccopy(s, n, at))
    for s in range(2):
        for a, b in allchips:
            dccopy(s, a * 4 + b, findex(a, b, 1)).wait_recv()

    part = jnp.dot(xt[0], dall[0].reshape(16 * BLOCK, BS), preferred_element_type=jnp.float32)
    part = part + jnp.dot(xt[1], dall[1].reshape(16 * BLOCK, BS), preferred_element_type=jnp.float32)
    gproj[...] = (part * SCALE).astype(jnp.bfloat16)
    for wait in pending:
        wait()


def shards(teacher, owner, proj_tiles, student_tiles):
    bf, f32 = jnp.bfloat16, jnp.float32
    vm, sem = pltpu.VMEM, pltpu.SemaphoreType.DMA
    gather = [sem((8,))] * 4 + [sem((16,))] * 6
    scratch = [
        vm((ROWS, 8192), bf), pltpu.SMEM((2, 256), jnp.int32), vm((BT, BS), bf), vm((BLOCK, BS), bf),
        vm((16, ROWS, BT), bf), vm((BLOCK, BT), f32), vm((8, 4, BLOCK, BT), bf),
        vm((256, 8, BS), f32), vm((256, 8, BT), f32), vm((384, BT), f32), vm((2, BT, 1536), bf),
        vm((8, BLOCK, BS), bf), vm((8, BLOCK, BS), bf), vm((8, BLOCK, BS), f32),
        vm((8, BLOCK, BS), bf), vm((8, BLOCK, BS), bf), vm((BLOCK, BS), f32),
        vm((BLOCK, BS), bf), vm((BLOCK, BS), bf), vm((BLOCK, BS), bf), vm((2, 128), f32),
        vm((32, 2, 128), f32), vm((2, 16, BLOCK, BS), bf),
        sem((4,)), sem((16,)), sem((16,)), gather,
        sem((8,)), sem((8,)), sem((8,)), sem((8,)), sem, sem, sem, sem,
        sem((32,)), sem((32,)), sem((16,)), sem((16,)), sem((16,)), sem((16,)),
        pltpu.SemaphoreType.REGULAR,
    ]
    whole = pl.BlockSpec(memory_space=pltpu.VMEM)
    anywhere = pl.BlockSpec(memory_space=pl.ANY)
    return pl.pallas_call(
        kernel,
        name="distill",
        out_shape=(jax.ShapeDtypeStruct((BT, BS), bf), jax.ShapeDtypeStruct((BLOCK, BS), bf)),
        in_specs=[anywhere] * 4,
        out_specs=(whole, whole),
        scratch_shapes=scratch,
        compiler_params=pltpu.CompilerParams(
            collective_id=0, has_side_effects=True, vmem_limit_bytes=60 * 2**20
        ),
    )(teacher, owner, proj_tiles, student_tiles)


def solution(mesh):
    placed = (P(("group", "dev"), None), P(), P("dev", None), P(("group", "dev"), None))
    return jax.shard_map(
        shards,
        mesh=mesh,
        in_specs=placed,
        out_specs=(P("dev", None), P(("group", "dev"), None)),
        check_vma=False,
    )
```

```python
import math

import jax
import jax.numpy as jnp
from jax import lax
from jax.experimental import pallas as pl
from jax.experimental.pallas import tpu as pltpu
from jax.sharding import PartitionSpec as P

MESH = pl.DeviceIdType.MESH
DS = 4096
EPS = 1e-06
HIGH = lax.Precision.HIGHEST
ROWS = 6
BLOCK = 96
HALF = BLOCK // 2
BT = 512
BS = 256
SCALE = 1.0 / math.sqrt(3072)


def flip(v, m):
    if m == 0:
        return v
    if m == 1:
        return v + 1 - 2 * (v % 2)
    if m == 2:
        return v + 2 - 4 * (v // 2)
    return 3 - v


def flip1(v, m):
    return 1 - v if m else v


def remote(src, dst, ss, rs, dev):
    return pltpu.make_async_remote_copy(
        src_ref=src, dst_ref=dst, send_sem=ss, recv_sem=rs, device_id=dev, device_id_type=MESH
    )


def kernel(
    teacher_in, owner_in, proj_in, student_in,
    gproj, gstud,
    teacher, owner, proj, sall,
    arecv, xa, xg, y3, x3, xs, xt, ycs, ycr, yown, cs, cr, pbuf, pall, pr, sr, es, ex, er, sc, dall,
    in_s, a_s, a_r, z_s, zu_r, zd_r, x_s, p_r, m_r, f_r, co_s, co_r, c_s, c_r, q_s, q_r,
    e_s, e_r, sh_s, sh_r, mate_r, k_s, k_r, far,
):
    g = lax.axis_index("group")
    d = lax.axis_index("dev")
    x, zl, y, c = d // 64, (d // 8) % 8, (d // 2) % 4, d % 2
    zk, z0 = zl // 2, zl % 2
    zz = g * 8 + zl

    def dev(x=x, zk=zk, z0=z0, y=y, c=c, g=g):
        return (g, ((x * 8 + zk * 2 + z0) * 4 + y) * 2 + c)

    def zdev(step):
        to = (zz + step) % 16
        return (to // 8, ((x * 8 + to % 8) * 4 + y) * 2 + c)

    f = z0 * 8 + y * 2 + c
    chips = [(a, b) for a in range(2) for b in range(4) if (a, b) != (0, 0)]
    fpeers = [(a, b, e) for a in range(2) for b in range(4) for e in range(2) if (a, b, e) != (0, 0, 0)]

    def fdev(a, b, e):
        return dev(z0=flip1(z0, a), y=flip(y, b), c=flip1(c, e))

    def findex(a, b, e):
        return flip1(z0, a) * 8 + flip(y, b) * 2 + flip1(c, e)

    xup, xdown = dev(x=(x + 1) % 4), dev(x=(x + 3) % 4)
    zup, zdown = zdev(2), zdev(14)
    here = g * 4 + zk
    mate, cross = dev(c=1 - c), dev(g=1 - g)
    left, right, opposite = (x + 3) % 4, (x + 1) % 4, (x + 2) % 4

    pending = []

    def begin(cp):
        cp.start()
        return cp

    def sent(ref, sem):
        pending.append(remote(ref, ref, sem, sem, mate).wait_send)

    def got(ref, sem):
        remote(ref, ref, sem, sem, mate).wait_recv()

    loads = [
        pltpu.make_async_copy(a, b, in_s.at[n])
        for n, (a, b) in enumerate(
            [(teacher_in, teacher), (owner_in, owner), (proj_in, proj), (student_in, sall.at[0, f])]
        )
    ]
    for cp in loads:
        cp.start()
    bar = pltpu.get_barrier_semaphore()

    def greet(to):
        pl.semaphore_signal(bar, inc=1, device_id=to, device_id_type=MESH)

    for step in (2, 14, 4, 12):
        greet(zdev(step))
    for a, b, e in fpeers:
        greet(fdev(a, b, e))
    greet(xup)
    greet(xdown)
    loads[0].wait()
    pl.semaphore_wait(bar, 21)
    pl.semaphore_signal(far, inc=1, device_id=zdev(4), device_id_type=MESH)

    for a, b, e in fpeers:
        to = findex(a, b, e)
        piece = teacher.at[:, pl.ds(pl.multiple_of(to * BT, BT), BT)]
        begin(remote(piece, arecv.at[f], a_s, a_r, fdev(a, b, e)))
    sent(arecv.at[0:15], a_s)
    arecv[f] = teacher[:, pl.ds(pl.multiple_of(f * BT, BT), BT)]

    def share(buf, s, n):
        for m, (a, b) in enumerate(chips):
            begin(remote(buf.at[s, f], buf.at[s, f], sh_s.at[n], sh_r.at[n * 7 + m], fdev(a, b, 0)))
        begin(remote(buf.at[s, f], buf.at[s, f], sh_s.at[n], mate_r.at[n], mate))
        sent(buf.at[s, 0:15], sh_s.at[n])

    def relay(buf, s, n):
        for m, (a, b) in enumerate(chips):
            block = buf.at[s, findex(a, b, 0)]
            got(block, sh_r.at[n * 7 + m])
            begin(remote(block, block, sh_s.at[n], mate_r.at[n], mate))

    def settle(buf, s, n):
        got(buf.at[s, 0:8], mate_r.at[n])

    for cp in loads[1:]:
        cp.wait()
    share(sall, 0, 0)
    got(arecv.at[0:15], a_r)
    for n in range(16):
        xa[n * ROWS : (n + 1) * ROWS, :] = arecv[n].astype(jnp.float32)
    xg[here, x] = xa[...].astype(jnp.bfloat16)

    def view(k, at, h):
        return xg.at[k, at, pl.ds(h * HALF, HALF)]

    def below(s):
        return (here + 8 - s) % 8

    def above(s):
        return (here + s) % 8

    def upcopy(s, h):
        v = view(below(s), x, h)
        return remote(v, v, z_s, zu_r.at[s * 2 + h], zup)

    def downcopy(s, h):
        v = view(above(s), x, h)
        return remote(v, v, z_s, zd_r.at[s * 2 + h], zdown)

    def pcopy(k, at, h):
        v = view(k, at, h)
        return remote(v, v, x_s, f_r.at[k] if h else p_r.at[k], xup)

    def mcopy(k, at, h):
        v = view(k, at, h)
        return remote(v, v, x_s, m_r.at[k] if h else f_r.at[k], xdown)

    def hcopy(k, at, h):
        v = view(k, at, h)
        return remote(v, v, x_s, f_r.at[k], xdown if h else xup)

    def xforward(k):
        pcopy(k, left, 0).wait_recv()
        begin(hcopy(k, left, 0))
        mcopy(k, right, 1).wait_recv()
        begin(hcopy(k, right, 1))

    def finish(k):
        got(xg.at[k, 0:2], f_r.at[k])

    def xsend(k, h):
        begin(pcopy(k, x, h))
        begin(mcopy(k, x, h))

    def zstep(s, h):
        if s < 4 or h == 0:
            got(view(below(s), x, h), zu_r.at[(s - 1) * 2 + h])
            if s < 3 or (s == 3 and h == 0):
                begin(upcopy(s, h))
        if s < 4 or h == 1:
            got(view(above(s), x, h), zd_r.at[(s - 1) * 2 + h])
            if s < 3 or (s == 3 and h == 1):
                begin(downcopy(s, h))

    edge = (zk == 0) | (zk == 3)
    first, second = [here], [here]
    for s in range(1, 4):
        up_first = zk + s <= 3
        first.append(jnp.where(up_first, above(s), below(s)))
        second.append(jnp.where(up_first, below(s), above(s)))
    far_block = above(4)
    inner = [here, first[1], jnp.where(edge, first[2], second[1]), jnp.where(edge, first[3], first[2])]
    outer = [jnp.where(edge, second[1], second[2]), jnp.where(edge, second[2], first[3]), second[3], far_block]

    def multiply(k):
        part = jnp.dot(
            xg[k].reshape(4 * BLOCK, BT), proj[...], preferred_element_type=jnp.float32
        )
        for i in range(4):
            for n in range(16):
                r = (i * 16 + n) * ROWS
                y3[(i * 4 + k % 4) * 16 + n, 0:ROWS, :] = part[r : r + ROWS, :]

    def spread(k):
        @pl.loop(0, 4)
        def _(i):
            block = xg[k, i].astype(jnp.float32)
            for n in range(16):
                x3[(i * 4 + k % 4) * 16 + n, 0:ROWS, :] = block[n * ROWS : (n + 1) * ROWS, :]

    def arrange(which, half, first, last):
        @pl.loop(first, last)
        def _(it):
            for j in range(4):
                for n in range(16):
                    r = (j * 16 + n) * ROWS
                    xs[r : r + ROWS, :] = x3[owner[half, (it * 4 + j) * 16 + n]][0:ROWS]
            for m in range(3):
                to = pl.ds(pl.multiple_of(it * 384 + m * 128, 128), 128)
                xt[which, :, to] = xs[m * 128 : (m + 1) * 128, :].T.astype(jnp.bfloat16)

    for h in range(2):
        begin(upcopy(0, h))
        begin(downcopy(0, h))
        xsend(here, h)
    zstep(1, 0)
    xsend(first[1], 0)
    xforward(here)
    zstep(1, 1)
    xsend(first[1], 1)
    xsend(second[1], 0)
    xsend(second[1], 1)
    zstep(2, 0)
    xsend(first[2], 0)
    xforward(first[1])
    zstep(2, 1)
    xsend(first[2], 1)
    xforward(second[1])
    finish(here)
    multiply(here)
    spread(here)
    zstep(3, 0)
    xsend(first[3], 0)
    xforward(first[2])
    zstep(3, 1)
    xsend(first[3], 1)
    xsend(second[2], 0)
    xsend(second[2], 1)
    finish(first[1])
    multiply(first[1])
    spread(first[1])
    xforward(first[3])
    xforward(second[2])
    xsend(second[3], 0)
    xsend(second[3], 1)
    finish(inner[2])
    multiply(inner[2])
    finish(inner[3])
    multiply(inner[3])

    def build(fi, put):
        for n in range(16):
            put(slice(n * ROWS, (n + 1) * ROWS), y3[owner[g, fi * 16 + n]][0:ROWS])

    def cocopy(j):
        return remote(ycs.at[j], ycr.at[j], co_s, co_r.at[j], mate)

    allchips = [(0, 0)] + chips
    order_c = chips + [(0, 0)]
    for a, b in order_c:
        j = a * 4 + b

        def put(rows, v):
            pbuf[rows, :] = v

        def keep(rows, v):
            yown[j, rows, :] = v

        build(findex(a, b, 1), put)
        ycs[j] = pbuf[...].astype(jnp.bfloat16)
        begin(cocopy(j))
        build(findex(a, b, 0), keep)

    def ccopy(a, b):
        j = a * 4 + b
        return remote(cs.at[j], cr.at[j], c_s, c_r, fdev(a, b, 0))

    for a, b in order_c:
        j = a * 4 + b
        cocopy(j).wait_recv()
        total = yown[j] + ycr[j].astype(jnp.float32)
        if j:
            cs[j] = total.astype(jnp.bfloat16)
            begin(ccopy(a, b))
        else:
            pbuf[...] = total

    pl.semaphore_wait(far, 1)
    begin(remote(sall.at[0, f], sr, q_s.at[0], q_r.at[0], cross))
    sent(sall.at[0, 0], q_s.at[0])
    sent(ycs, co_s)
    sent(cs.at[1:8], c_s)
    spread(inner[2])
    spread(inner[3])
    arrange(0, g, 0, 4)
    for h in range(2):
        zstep(4, h)
        xsend(far_block, h)
    xforward(second[3])
    relay(sall, 0, 0)

    got(cr.at[1:8], c_r)
    total = pbuf[...]
    for j in range(1, 8):
        total = total + cr[j].astype(jnp.float32)
    pbuf[...] = total

    target = sall[0, f].astype(jnp.float32)
    ones = jnp.ones((8, BS), jnp.float32)
    dims = (((1,), (1,)), ((), ()))
    sq = lax.dot_general(ones, total * total, dims, precision=HIGH, preferred_element_type=jnp.float32)
    sp = lax.dot_general(ones, total * target, dims, precision=HIGH, preferred_element_type=jnp.float32)
    which = lax.broadcasted_iota(jnp.int32, (2, BLOCK), 0)
    es[...] = jnp.zeros((2, 128), jnp.float32)
    es[:, 0:BLOCK] = jnp.where(which == 0, sq[0:2], sp[0:2])
    for m in range(1, 4):
        begin(remote(es, ex.at[m], e_s.at[0], e_r.at[0], dev(x=flip(x, m))))
    sent(ex.at[1:4], e_s.at[0])
    pall[0, f] = total.astype(jnp.bfloat16)
    begin(remote(pall.at[0, f], pr, q_s.at[1], q_r.at[1], cross))
    sent(pall.at[0, 0], q_s.at[1])
    got(ex.at[1:4], e_r.at[0])
    er[here] = es[...] + ex[1] + ex[2] + ex[3]
    for m in (4, 3, 5, 2, 6, 1, 7):
        begin(remote(er.at[here], er.at[here], e_s.at[1], e_r.at[1], zdev(2 * m)))
    sent(er.at[0:7], e_s.at[1])
    share(pall, 0, 1)
    xforward(far_block)
    for k in outer:
        finish(k)
        spread(k)
    arrange(1, 1 - g, 0, 4)
    sent(xg.at[0:7, 0], z_s)
    sent(xg.at[0:6], x_s)
    got(sr, q_r.at[0])
    got(pr, q_r.at[1])

    got(er.at[0:7], e_r.at[1])
    sums = []
    for base in (g * 4, (1 - g) * 4):
        sums.append(er[base] + er[base + 1] + er[base + 2] + er[base + 3])
    factors = []
    for v in sums:
        sq, sp = v[0:1], v[1:2]
        root = jnp.sqrt(sq / DS + EPS)
        inner_mean = (sq / (root * root) - sp / root) / DS
        factors.append(((1.0 - inner_mean) / (root * root), 1.0 / root))
    sc[f] = jnp.concatenate(factors[0], axis=0)
    for a, b, e in fpeers:
        begin(remote(sc.at[f], sc.at[f], k_s, k_r, fdev(a, b, e)))
    sent(sc.at[0:15], k_s)

    def column(v):
        return jnp.broadcast_to(v, (128, 128)).T[0:BLOCK]

    def slope(state, tile, one, two):
        return (state.astype(jnp.float32) * one - tile.astype(jnp.float32) * two).astype(jnp.bfloat16)

    halves = [slice(m * 128, (m + 1) * 128) for m in range(2)]
    one, two = column(factors[1][0]), column(factors[1][1])
    for lanes in halves:
        dall[1, f, :, lanes] = slope(pr[:, lanes], sr[:, lanes], one, two)
    share(dall, 1, 2)
    relay(pall, 0, 1)
    two = column(factors[0][1])
    for lanes in halves:
        gstud[:, lanes] = (target[:, lanes] - pbuf[:, lanes] * two).astype(jnp.bfloat16)
    settle(sall, 0, 0)
    settle(pall, 0, 1)
    got(sc.at[0:15], k_r)

    @pl.loop(0, 16)
    def _(n):
        rows = sc[n]
        one, two = column(rows[0:1]), column(rows[1:2])
        for lanes in halves:
            dall[0, n, :, lanes] = slope(pall[0, n, :, lanes], sall[0, n, :, lanes], one, two)

    relay(dall, 1, 2)
    settle(dall, 1, 2)

    part = jnp.dot(xt[0], dall[0].reshape(16 * BLOCK, BS), preferred_element_type=jnp.float32)
    part = part + jnp.dot(xt[1], dall[1].reshape(16 * BLOCK, BS), preferred_element_type=jnp.float32)
    gproj[...] = (part * SCALE).astype(jnp.bfloat16)
    for wait in pending:
        wait()


def shards(teacher, owner, proj_tiles, student_tiles):
    bf, f32 = jnp.bfloat16, jnp.float32
    vm, sem = pltpu.VMEM, pltpu.SemaphoreType.DMA
    one, pair = vm((1, 16, BLOCK, BS), bf), vm((2, 16, BLOCK, BS), bf)
    tile = vm((BLOCK, BS), bf)
    scratch = [
        vm((ROWS, 8192), bf), pltpu.SMEM((2, 256), jnp.int32), vm((BT, BS), bf), one,
        vm((16, ROWS, BT), bf), vm((BLOCK, BT), f32), vm((8, 4, BLOCK, BT), bf),
        vm((256, 8, BS), f32), vm((256, 8, BT), f32), vm((384, BT), f32), vm((2, BT, 1536), bf),
        vm((8, BLOCK, BS), bf), vm((8, BLOCK, BS), bf), vm((8, BLOCK, BS), f32),
        vm((8, BLOCK, BS), bf), vm((8, BLOCK, BS), bf), vm((BLOCK, BS), f32),
        one, tile, tile, vm((2, 128), f32), vm((4, 2, 128), f32), vm((8, 2, 128), f32), vm((16, 2, 128), f32), pair,
        sem((4,)), sem, sem, sem, sem((8,)), sem((8,)), sem, sem((8,)), sem((8,)), sem((8,)),
        sem, sem((8,)), sem, sem, sem((2,)), sem((2,)),
        sem((2,)), sem((2,)), sem((3,)), sem((21,)), sem((3,)), sem, sem,
        pltpu.SemaphoreType.REGULAR,
    ]
    whole = pl.BlockSpec(memory_space=pltpu.VMEM)
    anywhere = pl.BlockSpec(memory_space=pltpu.HBM)
    return pl.pallas_call(
        kernel,
        name="distill",
        out_shape=(jax.ShapeDtypeStruct((BT, BS), bf), jax.ShapeDtypeStruct((BLOCK, BS), bf)),
        in_specs=[anywhere] * 4,
        out_specs=(whole, whole),
        scratch_shapes=scratch,
        compiler_params=pltpu.CompilerParams(
            collective_id=0, has_side_effects=True, vmem_limit_bytes=60 * 2**20
        ),
    )(teacher, owner, proj_tiles, student_tiles)


def solution(mesh):
    placed = (P(("group", "dev"), None), P(), P("dev", None), P(("group", "dev"), None))
    return jax.shard_map(
        shards,
        mesh=mesh,
        in_specs=placed,
        out_specs=(P("dev", None), P(("group", "dev"), None)),
        check_vma=False,
    )
```

```python
import math

import jax
import jax.numpy as jnp
from jax import lax
from jax.experimental import pallas as pl
from jax.experimental.pallas import tpu as pltpu
from jax.sharding import PartitionSpec as P

MESH = pl.DeviceIdType.MESH
DS = 4096
EPS = 1e-06
HIGH = lax.Precision.HIGHEST
ROWS = 6
BLOCK = 96
HALF = BLOCK // 2
BT = 512
BS = 256
SCALE = 1.0 / math.sqrt(3072)


def flip(v, m):
    if m == 0:
        return v
    if m == 1:
        return v + 1 - 2 * (v % 2)
    if m == 2:
        return v + 2 - 4 * (v // 2)
    return 3 - v


def flip1(v, m):
    return 1 - v if m else v


def remote(src, dst, ss, rs, dev):
    return pltpu.make_async_remote_copy(
        src_ref=src, dst_ref=dst, send_sem=ss, recv_sem=rs, device_id=dev, device_id_type=MESH
    )


def kernel(
    teacher_in, owner_in, proj_in, student_in,
    gproj, gstud,
    teacher, owner, proj, sall,
    arecv, xa, xg, y3, x3, xs, xt, ycs, ycr, yown, cs, cr, pbuf, pall, pr, sr, es, ex, er, sc, dall,
    in_s, a_s, a_r, z_s, end_s, zu_r, zd_r, x_s, p_r, m_r, f_r, co_s, co_r, c_s, c_r, q_s, q_r,
    e_s, e_r, sh_s, sh_r, mate_r, k_s, k_r, far,
):
    g = lax.axis_index("group")
    d = lax.axis_index("dev")
    x, zl, y, c = d // 64, (d // 8) % 8, (d // 2) % 4, d % 2
    zk, z0 = zl // 2, zl % 2
    zz = g * 8 + zl

    def dev(x=x, zk=zk, z0=z0, y=y, c=c, g=g):
        return (g, ((x * 8 + zk * 2 + z0) * 4 + y) * 2 + c)

    def zdev(step):
        to = (zz + step) % 16
        return (to // 8, ((x * 8 + to % 8) * 4 + y) * 2 + c)

    f = z0 * 8 + y * 2 + c
    chips = [(a, b) for a in range(2) for b in range(4) if (a, b) != (0, 0)]
    fpeers = [(a, b, e) for a in range(2) for b in range(4) for e in range(2) if (a, b, e) != (0, 0, 0)]

    def fdev(a, b, e):
        return dev(z0=flip1(z0, a), y=flip(y, b), c=flip1(c, e))

    def findex(a, b, e):
        return flip1(z0, a) * 8 + flip(y, b) * 2 + flip1(c, e)

    xup, xdown = dev(x=(x + 1) % 4), dev(x=(x + 3) % 4)
    zup, zdown = zdev(2), zdev(14)
    here = g * 4 + zk
    mate, cross = dev(c=1 - c), dev(g=1 - g)
    left, right, opposite = (x + 3) % 4, (x + 1) % 4, (x + 2) % 4

    pending = []

    def begin(cp):
        cp.start()
        return cp

    def sent(ref, sem):
        pending.append(remote(ref, ref, sem, sem, mate).wait_send)

    def got(ref, sem):
        remote(ref, ref, sem, sem, mate).wait_recv()

    loads = [
        pltpu.make_async_copy(a, b, in_s.at[n])
        for n, (a, b) in enumerate(
            [(teacher_in, teacher), (owner_in, owner), (proj_in, proj), (student_in, sall.at[0, f])]
        )
    ]
    for cp in loads:
        cp.start()
    bar = pltpu.get_barrier_semaphore()

    def greet(to):
        pl.semaphore_signal(bar, inc=1, device_id=to, device_id_type=MESH)

    for step in (2, 14, 4, 12):
        greet(zdev(step))
    for a, b, e in fpeers:
        greet(fdev(a, b, e))
    greet(xup)
    greet(xdown)
    loads[0].wait()

    edge = (zk == 0) | (zk == 3)
    end = zdev(jnp.where(zk == 0, 6, 10))

    @pl.when(edge)
    def _():
        greet(end)

    pl.semaphore_wait(bar, 21 + jnp.where(edge, 1, 0))
    pl.semaphore_signal(far, inc=1, device_id=zdev(4), device_id_type=MESH)

    for a, b, e in fpeers:
        to = findex(a, b, e)
        piece = teacher.at[:, pl.ds(pl.multiple_of(to * BT, BT), BT)]
        begin(remote(piece, arecv.at[f], a_s, a_r, fdev(a, b, e)))
    sent(arecv.at[0:15], a_s)
    arecv[f] = teacher[:, pl.ds(pl.multiple_of(f * BT, BT), BT)]

    def share(buf, s, n):
        for m, (a, b) in enumerate(chips):
            begin(remote(buf.at[s, f], buf.at[s, f], sh_s.at[n], sh_r.at[n * 7 + m], fdev(a, b, 0)))
        begin(remote(buf.at[s, f], buf.at[s, f], sh_s.at[n], mate_r.at[n], mate))
        sent(buf.at[s, 0:15], sh_s.at[n])

    def relay(buf, s, n):
        for m, (a, b) in enumerate(chips):
            block = buf.at[s, findex(a, b, 0)]
            got(block, sh_r.at[n * 7 + m])
            begin(remote(block, block, sh_s.at[n], mate_r.at[n], mate))

    def settle(buf, s, n):
        got(buf.at[s, 0:8], mate_r.at[n])

    for cp in loads[1:]:
        cp.wait()
    got(arecv.at[0:15], a_r)
    for n in range(16):
        xa[n * ROWS : (n + 1) * ROWS, :] = arecv[n].astype(jnp.float32)
    xg[here, x] = xa[...].astype(jnp.bfloat16)

    def view(k, at, h):
        return xg.at[k, at, pl.ds(h * HALF, HALF)]

    def below(s):
        return (here + 8 - s) % 8

    def above(s):
        return (here + s) % 8

    def upcopy(s, h):
        v = view(below(s), x, h)
        return remote(v, v, z_s, zu_r.at[s * 2 + h], zup)

    def downcopy(s, h):
        v = view(above(s), x, h)
        return remote(v, v, z_s, zd_r.at[s * 2 + h], zdown)

    def pcopy(k, at, h):
        v = view(k, at, h)
        return remote(v, v, x_s, f_r.at[k] if h else p_r.at[k], xup)

    def mcopy(k, at, h):
        v = view(k, at, h)
        return remote(v, v, x_s, m_r.at[k] if h else f_r.at[k], xdown)

    def hcopy(k, at, h):
        v = view(k, at, h)
        return remote(v, v, x_s, f_r.at[k], xdown if h else xup)

    def xforward(k):
        pcopy(k, left, 0).wait_recv()
        begin(hcopy(k, left, 0))
        mcopy(k, right, 1).wait_recv()
        begin(hcopy(k, right, 1))

    def finish(k):
        got(xg.at[k, 0:2], f_r.at[k])

    def xsend(k, h):
        begin(pcopy(k, x, h))
        begin(mcopy(k, x, h))

    def xsend_if(cond, k):
        @pl.when(cond)
        def _():
            xsend(k, 0)
            xsend(k, 1)

    def zstep(s, h):
        if s < 4 or h == 0:
            if s == 3:
                pl.when(zk != 3)(lambda: got(view(below(s), x, h), zu_r.at[4 + h]))
            else:
                got(view(below(s), x, h), zu_r.at[(s - 1) * 2 + h])
            if s == 2:
                pl.when(zk != 2)(upcopy(s, h).start)
            elif s < 2 or (s == 3 and h == 0):
                begin(upcopy(s, h))
        if s < 4 or h == 1:
            if s == 3:
                pl.when(zk != 0)(lambda: got(view(above(s), x, h), zd_r.at[4 + h]))
            else:
                got(view(above(s), x, h), zd_r.at[(s - 1) * 2 + h])
            if s == 2:
                pl.when(zk != 1)(downcopy(s, h).start)
            elif s < 2 or (s == 3 and h == 1):
                begin(downcopy(s, h))

    def ends_send():
        for h in range(2):
            v = view(here, x, h)
            pl.when(zk == 0)(remote(v, v, end_s, zu_r.at[4 + h], end).start)
            pl.when(zk == 3)(remote(v, v, end_s, zd_r.at[4 + h], end).start)

    def ends_arrive():
        for h in range(2):

            @pl.when(zk == 3)
            def _():
                got(view(below(3), x, h), zu_r.at[4 + h])
                xsend(below(3), h)

            @pl.when(zk == 0)
            def _():
                got(view(above(3), x, h), zd_r.at[4 + h])
                xsend(above(3), h)

    first, second = [here], [here]
    for s in range(1, 4):
        up_first = zk + s <= 3
        first.append(jnp.where(up_first, above(s), below(s)))
        second.append(jnp.where(up_first, below(s), above(s)))
    far_block = above(4)
    inner = [here, first[1], jnp.where(edge, first[2], second[1]), jnp.where(edge, first[3], first[2])]
    outer = [jnp.where(edge, second[1], second[2]), jnp.where(edge, second[2], first[3]), second[3], far_block]

    def multiply(k):
        part = jnp.dot(
            xg[k].reshape(4 * BLOCK, BT), proj[...], preferred_element_type=jnp.float32
        )
        for i in range(4):
            for n in range(16):
                r = (i * 16 + n) * ROWS
                y3[(i * 4 + k % 4) * 16 + n, 0:ROWS, :] = part[r : r + ROWS, :]

    def spread(k):
        @pl.loop(0, 4)
        def _(i):
            block = xg[k, i].astype(jnp.float32)
            for n in range(16):
                x3[(i * 4 + k % 4) * 16 + n, 0:ROWS, :] = block[n * ROWS : (n + 1) * ROWS, :]

    def arrange(which, half, first, last):
        @pl.loop(first, last)
        def _(it):
            for j in range(4):
                for n in range(16):
                    r = (j * 16 + n) * ROWS
                    xs[r : r + ROWS, :] = x3[owner[half, (it * 4 + j) * 16 + n]][0:ROWS]
            for m in range(3):
                to = pl.ds(pl.multiple_of(it * 384 + m * 128, 128), 128)
                xt[which, :, to] = xs[m * 128 : (m + 1) * 128, :].T.astype(jnp.bfloat16)

    for h in range(2):
        begin(upcopy(0, h))
        begin(downcopy(0, h))
        xsend(here, h)
    ends_send()
    zstep(1, 0)
    xsend(first[1], 0)
    xforward(here)
    zstep(1, 1)
    xsend(first[1], 1)
    inside = jnp.logical_not(edge)
    xsend_if(inside, second[1])
    zstep(2, 0)
    xsend(first[2], 0)
    xforward(first[1])
    zstep(2, 1)
    xsend(first[2], 1)
    finish(here)
    multiply(here)
    spread(here)
    pl.semaphore_wait(far, 1)
    begin(remote(sall.at[0, f], sr, q_s.at[0], q_r.at[0], cross))
    sent(sall.at[0, 0], q_s.at[0])
    ends_arrive()
    xforward(inner[2])
    finish(first[1])
    multiply(first[1])
    spread(first[1])
    xforward(inner[3])
    zstep(3, 0)
    zstep(3, 1)
    xsend(outer[0], 0)
    xsend(outer[0], 1)
    finish(inner[2])
    multiply(inner[2])
    finish(inner[3])
    multiply(inner[3])

    def build(fi, put):
        for n in range(16):
            put(slice(n * ROWS, (n + 1) * ROWS), y3[owner[g, fi * 16 + n]][0:ROWS])

    def cocopy(j):
        return remote(ycs.at[j], ycr.at[j], co_s, co_r.at[j], mate)

    allchips = [(0, 0)] + chips
    order_c = chips + [(0, 0)]
    for a, b in order_c:
        j = a * 4 + b

        def put(rows, v):
            pbuf[rows, :] = v

        def keep(rows, v):
            yown[j, rows, :] = v

        build(findex(a, b, 1), put)
        ycs[j] = pbuf[...].astype(jnp.bfloat16)
        begin(cocopy(j))
        build(findex(a, b, 0), keep)

    def ccopy(a, b):
        j = a * 4 + b
        return remote(cs.at[j], cr.at[j], c_s, c_r, fdev(a, b, 0))

    for a, b in order_c:
        j = a * 4 + b
        cocopy(j).wait_recv()
        total = yown[j] + ycr[j].astype(jnp.float32)
        if j:
            cs[j] = total.astype(jnp.bfloat16)
            begin(ccopy(a, b))
        else:
            pbuf[...] = total

    share(sall, 0, 0)
    sent(ycs, co_s)
    sent(cs.at[1:8], c_s)
    spread(inner[2])
    spread(inner[3])
    arrange(0, g, 0, 4)
    xsend(outer[1], 0)
    xsend(outer[1], 1)
    for h in range(2):
        zstep(4, h)

    got(cr.at[1:8], c_r)
    total = pbuf[...]
    for j in range(1, 8):
        total = total + cr[j].astype(jnp.float32)
    pbuf[...] = total

    target = sall[0, f].astype(jnp.float32)
    ones = jnp.ones((8, BS), jnp.float32)
    dims = (((1,), (1,)), ((), ()))
    sq = lax.dot_general(ones, total * total, dims, precision=HIGH, preferred_element_type=jnp.float32)
    sp = lax.dot_general(ones, total * target, dims, precision=HIGH, preferred_element_type=jnp.float32)
    which = lax.broadcasted_iota(jnp.int32, (2, BLOCK), 0)
    es[...] = jnp.zeros((2, 128), jnp.float32)
    es[:, 0:BLOCK] = jnp.where(which == 0, sq[0:2], sp[0:2])
    for m in range(1, 4):
        begin(remote(es, ex.at[m], e_s.at[0], e_r.at[0], dev(x=flip(x, m))))
    sent(ex.at[1:4], e_s.at[0])
    pall[0, f] = total.astype(jnp.bfloat16)
    begin(remote(pall.at[0, f], pr, q_s.at[1], q_r.at[1], cross))
    sent(pall.at[0, 0], q_s.at[1])
    xforward(outer[0])
    xforward(outer[1])
    got(ex.at[1:4], e_r.at[0])
    er[here] = es[...] + ex[1] + ex[2] + ex[3]
    for m in (4, 3, 5, 2, 6, 1, 7):
        begin(remote(er.at[here], er.at[here], e_s.at[1], e_r.at[1], zdev(2 * m)))
    sent(er.at[0:7], e_s.at[1])
    share(pall, 0, 1)
    for k in outer[2:]:
        xsend(k, 0)
        xsend(k, 1)
    for k in outer[:2]:
        finish(k)
        spread(k)
    relay(sall, 0, 0)
    got(sr, q_r.at[0])
    for k in outer[2:]:
        xforward(k)
    got(pr, q_r.at[1])

    got(er.at[0:7], e_r.at[1])
    sums = []
    for base in (g * 4, (1 - g) * 4):
        sums.append(er[base] + er[base + 1] + er[base + 2] + er[base + 3])
    factors = []
    for v in sums:
        sq, sp = v[0:1], v[1:2]
        root = jnp.sqrt(sq / DS + EPS)
        inner_mean = (sq / (root * root) - sp / root) / DS
        factors.append(((1.0 - inner_mean) / (root * root), 1.0 / root))
    sc[f] = jnp.concatenate(factors[0], axis=0)
    for a, b, e in fpeers:
        begin(remote(sc.at[f], sc.at[f], k_s, k_r, fdev(a, b, e)))
    sent(sc.at[0:15], k_s)

    def column(v):
        return jnp.broadcast_to(v, (128, 128)).T[0:BLOCK]

    def slope(state, tile, one, two):
        return (state.astype(jnp.float32) * one - tile.astype(jnp.float32) * two).astype(jnp.bfloat16)

    halves = [slice(m * 128, (m + 1) * 128) for m in range(2)]
    one, two = column(factors[1][0]), column(factors[1][1])
    for lanes in halves:
        dall[1, f, :, lanes] = slope(pr[:, lanes], sr[:, lanes], one, two)
    share(dall, 1, 2)
    for k in outer[2:]:
        finish(k)
        spread(k)
    arrange(1, 1 - g, 0, 4)
    def z_sent():
        block = lambda n: xg.at[0:n, 0]
        pl.when(edge)(remote(block(7), block(7), z_s, z_s, mate).wait_send)
        pl.when(edge)(remote(block(1), block(1), end_s, end_s, mate).wait_send)
        pl.when(inside)(remote(block(6), block(6), z_s, z_s, mate).wait_send)

    pending.append(z_sent)
    sent(xg.at[0:6], x_s)
    relay(pall, 0, 1)
    two = column(factors[0][1])
    for lanes in halves:
        gstud[:, lanes] = (target[:, lanes] - pbuf[:, lanes] * two).astype(jnp.bfloat16)
    settle(sall, 0, 0)
    settle(pall, 0, 1)
    got(sc.at[0:15], k_r)

    @pl.loop(0, 16)
    def _(n):
        rows = sc[n]
        one, two = column(rows[0:1]), column(rows[1:2])
        for lanes in halves:
            dall[0, n, :, lanes] = slope(pall[0, n, :, lanes], sall[0, n, :, lanes], one, two)

    relay(dall, 1, 2)
    settle(dall, 1, 2)

    part = jnp.dot(xt[0], dall[0].reshape(16 * BLOCK, BS), preferred_element_type=jnp.float32)
    part = part + jnp.dot(xt[1], dall[1].reshape(16 * BLOCK, BS), preferred_element_type=jnp.float32)
    gproj[...] = (part * SCALE).astype(jnp.bfloat16)
    for wait in pending:
        wait()


def shards(teacher, owner, proj_tiles, student_tiles):
    bf, f32 = jnp.bfloat16, jnp.float32
    vm, sem = pltpu.VMEM, pltpu.SemaphoreType.DMA
    one, pair = vm((1, 16, BLOCK, BS), bf), vm((2, 16, BLOCK, BS), bf)
    tile = vm((BLOCK, BS), bf)
    scratch = [
        vm((ROWS, 8192), bf), pltpu.SMEM((2, 256), jnp.int32), vm((BT, BS), bf), one,
        vm((16, ROWS, BT), bf), vm((BLOCK, BT), f32), vm((8, 4, BLOCK, BT), bf),
        vm((256, 8, BS), f32), vm((256, 8, BT), f32), vm((384, BT), f32), vm((2, BT, 1536), bf),
        vm((8, BLOCK, BS), bf), vm((8, BLOCK, BS), bf), vm((8, BLOCK, BS), f32),
        vm((8, BLOCK, BS), bf), vm((8, BLOCK, BS), bf), vm((BLOCK, BS), f32),
        one, tile, tile, vm((2, 128), f32), vm((4, 2, 128), f32), vm((8, 2, 128), f32), vm((16, 2, 128), f32), pair,
        sem((4,)), sem, sem, sem, sem, sem((8,)), sem((8,)), sem, sem((8,)), sem((8,)), sem((8,)),
        sem, sem((8,)), sem, sem, sem((2,)), sem((2,)),
        sem((2,)), sem((2,)), sem((3,)), sem((21,)), sem((3,)), sem, sem,
        pltpu.SemaphoreType.REGULAR,
    ]
    whole = pl.BlockSpec(memory_space=pltpu.VMEM)
    anywhere = pl.BlockSpec(memory_space=pltpu.HBM)
    return pl.pallas_call(
        kernel,
        name="distill",
        out_shape=(jax.ShapeDtypeStruct((BT, BS), bf), jax.ShapeDtypeStruct((BLOCK, BS), bf)),
        in_specs=[anywhere] * 4,
        out_specs=(whole, whole),
        scratch_shapes=scratch,
        compiler_params=pltpu.CompilerParams(
            collective_id=0, has_side_effects=True, vmem_limit_bytes=36 * 2**20
        ),
    )(*(pltpu.with_memory_space_constraint(v, pltpu.HBM) for v in (teacher, owner, proj_tiles, student_tiles)))


def solution(mesh):
    placed = (P(("group", "dev"), None), P(), P("dev", None), P(("group", "dev"), None))
    return jax.shard_map(
        shards,
        mesh=mesh,
        in_specs=placed,
        out_specs=(P("dev", None), P(("group", "dev"), None)),
        check_vma=False,
    )
```

```python
import math

import jax
import jax.numpy as jnp
from jax import lax
from jax.experimental import pallas as pl
from jax.experimental.pallas import tpu as pltpu
from jax.sharding import PartitionSpec as P

MESH = pl.DeviceIdType.MESH
DS = 4096
EPS = 1e-06
HIGH = lax.Precision.HIGHEST
ROWS = 6
BLOCK = 96
HALF = BLOCK // 2
BT = 512
BS = 256
SCALE = 1.0 / math.sqrt(3072)


def flip(v, m):
    if m == 0:
        return v
    if m == 1:
        return v + 1 - 2 * (v % 2)
    if m == 2:
        return v + 2 - 4 * (v // 2)
    return 3 - v


def flip1(v, m):
    return 1 - v if m else v


def remote(src, dst, ss, rs, dev):
    return pltpu.make_async_remote_copy(
        src_ref=src, dst_ref=dst, send_sem=ss, recv_sem=rs, device_id=dev, device_id_type=MESH
    )


def kernel(
    teacher_in, owner_in, proj_in, student_in,
    gproj, gstud,
    teacher, owner, proj, sall,
    arecv, xa, xg, y3, x3, xs, xt, ycs, ycr, yown, cs, cr, pbuf, pall, pr, sr, es, ex, er, sc, dall,
    in_s, a_s, a_r, z_s, end_s, zu_r, zd_r, x_s, p_r, m_r, f_r, co_s, co_r, c_s, c_r, q_s, q_r,
    e_s, e_r, sh_s, sh_r, mate_r, k_s, k_r, far, back,
):
    g = lax.axis_index("group")
    d = lax.axis_index("dev")
    x, zl, y, c = d // 64, (d // 8) % 8, (d // 2) % 4, d % 2
    zk, z0 = zl // 2, zl % 2
    zz = g * 8 + zl

    def dev(x=x, zk=zk, z0=z0, y=y, c=c, g=g):
        return (g, ((x * 8 + zk * 2 + z0) * 4 + y) * 2 + c)

    def zdev(step):
        to = (zz + step) % 16
        return (to // 8, ((x * 8 + to % 8) * 4 + y) * 2 + c)

    f = z0 * 8 + y * 2 + c
    chips = [(a, b) for a in range(2) for b in range(4) if (a, b) != (0, 0)]
    fpeers = [(a, b, e) for a in range(2) for b in range(4) for e in range(2) if (a, b, e) != (0, 0, 0)]

    def fdev(a, b, e):
        return dev(z0=flip1(z0, a), y=flip(y, b), c=flip1(c, e))

    def findex(a, b, e):
        return flip1(z0, a) * 8 + flip(y, b) * 2 + flip1(c, e)

    xup, xdown = dev(x=(x + 1) % 4), dev(x=(x + 3) % 4)
    zup, zdown = zdev(2), zdev(14)
    here = g * 4 + zk
    mate, cross = dev(c=1 - c), dev(g=1 - g)
    left, right, opposite = (x + 3) % 4, (x + 1) % 4, (x + 2) % 4

    pending = []

    def begin(cp):
        cp.start()
        return cp

    def sent(ref, sem):
        pending.append(remote(ref, ref, sem, sem, mate).wait_send)

    def got(ref, sem):
        remote(ref, ref, sem, sem, mate).wait_recv()

    loads = [
        pltpu.make_async_copy(a, b, in_s.at[n])
        for n, (a, b) in enumerate(
            [(teacher_in, teacher), (owner_in, owner), (proj_in, proj), (student_in, sall.at[0, f])]
        )
    ]
    for cp in loads:
        cp.start()
    bar = pltpu.get_barrier_semaphore()

    def greet(to):
        pl.semaphore_signal(bar, inc=1, device_id=to, device_id_type=MESH)

    for step in (2, 14, 4, 12):
        greet(zdev(step))
    for a, b, e in fpeers:
        greet(fdev(a, b, e))
    greet(xup)
    greet(xdown)
    loads[0].wait()

    edge = (zk == 0) | (zk == 3)
    end = zdev(jnp.where(zk == 0, 6, 10))
    pl.semaphore_wait(bar, 21)
    pl.semaphore_signal(far, inc=1, device_id=zdev(4), device_id_type=MESH)
    pl.semaphore_signal(back, inc=1, device_id=zdev(12), device_id_type=MESH)

    for a, b, e in fpeers:
        to = findex(a, b, e)
        piece = teacher.at[:, pl.ds(pl.multiple_of(to * BT, BT), BT)]
        begin(remote(piece, arecv.at[f], a_s, a_r, fdev(a, b, e)))
    sent(arecv.at[0:15], a_s)
    arecv[f] = teacher[:, pl.ds(pl.multiple_of(f * BT, BT), BT)]

    def share(buf, s, n):
        for m, (a, b) in enumerate(chips):
            begin(remote(buf.at[s, f], buf.at[s, f], sh_s.at[n], sh_r.at[n * 7 + m], fdev(a, b, 0)))
        begin(remote(buf.at[s, f], buf.at[s, f], sh_s.at[n], mate_r.at[n], mate))
        sent(buf.at[s, 0:15], sh_s.at[n])

    def relay(buf, s, n):
        for m, (a, b) in enumerate(chips):
            block = buf.at[s, findex(a, b, 0)]
            got(block, sh_r.at[n * 7 + m])
            begin(remote(block, block, sh_s.at[n], mate_r.at[n], mate))

    def settle(buf, s, n):
        got(buf.at[s, 0:8], mate_r.at[n])

    for cp in loads[1:]:
        cp.wait()
    got(arecv.at[0:15], a_r)
    for n in range(16):
        xa[n * ROWS : (n + 1) * ROWS, :] = arecv[n].astype(jnp.float32)
    xg[here, x] = xa[...].astype(jnp.bfloat16)

    def view(k, at, h):
        return xg.at[k, at, pl.ds(h * HALF, HALF)]

    def below(s):
        return (here + 8 - s) % 8

    def above(s):
        return (here + s) % 8

    def upcopy(s, h):
        v = view(below(s), x, h)
        return remote(v, v, z_s, zu_r.at[s * 2 + h], zup)

    def downcopy(s, h):
        v = view(above(s), x, h)
        return remote(v, v, z_s, zd_r.at[s * 2 + h], zdown)

    def pcopy(k, at, h):
        v = view(k, at, h)
        return remote(v, v, x_s, f_r.at[k] if h else p_r.at[k], xup)

    def mcopy(k, at, h):
        v = view(k, at, h)
        return remote(v, v, x_s, m_r.at[k] if h else f_r.at[k], xdown)

    def hcopy(k, at, h):
        v = view(k, at, h)
        return remote(v, v, x_s, f_r.at[k], xdown if h else xup)

    def xforward(k):
        pcopy(k, left, 0).wait_recv()
        begin(hcopy(k, left, 0))
        mcopy(k, right, 1).wait_recv()
        begin(hcopy(k, right, 1))

    def finish(k):
        got(xg.at[k, 0:2], f_r.at[k])

    def xsend(k, h):
        begin(pcopy(k, x, h))
        begin(mcopy(k, x, h))

    def xsend_if(cond, k):
        @pl.when(cond)
        def _():
            xsend(k, 0)
            xsend(k, 1)

    def zstep(s, h):
        if s < 4 or h == 0:
            if s == 3:
                pl.when(zk != 3)(lambda: got(view(below(s), x, h), zu_r.at[4 + h]))
            else:
                got(view(below(s), x, h), zu_r.at[(s - 1) * 2 + h])
            if s == 2:
                pl.when(zk != 2)(upcopy(s, h).start)
            elif s < 2 or (s == 3 and h == 0):
                begin(upcopy(s, h))
        if s < 4 or h == 1:
            if s == 3:
                pl.when(zk != 0)(lambda: got(view(above(s), x, h), zd_r.at[4 + h]))
            else:
                got(view(above(s), x, h), zd_r.at[(s - 1) * 2 + h])
            if s == 2:
                pl.when(zk != 1)(downcopy(s, h).start)
            elif s < 2 or (s == 3 and h == 1):
                begin(downcopy(s, h))

    def ends_send():
        for h in range(2):
            v = view(here, x, h)
            pl.when(zk == 0)(remote(v, v, end_s, zu_r.at[4 + h], end).start)
            pl.when(zk == 3)(remote(v, v, end_s, zd_r.at[4 + h], end).start)

    def ends_arrive():
        for h in range(2):

            @pl.when(zk == 3)
            def _():
                got(view(below(3), x, h), zu_r.at[4 + h])
                xsend(below(3), h)

            @pl.when(zk == 0)
            def _():
                got(view(above(3), x, h), zd_r.at[4 + h])
                xsend(above(3), h)

    first, second = [here], [here]
    for s in range(1, 4):
        up_first = zk + s <= 3
        first.append(jnp.where(up_first, above(s), below(s)))
        second.append(jnp.where(up_first, below(s), above(s)))
    far_block = above(4)
    inner = [here, first[1], jnp.where(edge, first[2], second[1]), jnp.where(edge, first[3], first[2])]
    outer = [jnp.where(edge, second[1], second[2]), jnp.where(edge, second[2], first[3]), second[3], far_block]

    def multiply(k):
        part = jnp.dot(
            xg[k].reshape(4 * BLOCK, BT), proj[...], preferred_element_type=jnp.float32
        )
        for i in range(4):
            for n in range(16):
                r = (i * 16 + n) * ROWS
                y3[(i * 4 + k % 4) * 16 + n, 0:ROWS, :] = part[r : r + ROWS, :]

    def spread(k):
        @pl.loop(0, 4)
        def _(i):
            block = xg[k, i].astype(jnp.float32)
            for n in range(16):
                x3[(i * 4 + k % 4) * 16 + n, 0:ROWS, :] = block[n * ROWS : (n + 1) * ROWS, :]

    def arrange(which, half, first, last):
        @pl.loop(first, last)
        def _(it):
            for j in range(4):
                for n in range(16):
                    r = (j * 16 + n) * ROWS
                    xs[r : r + ROWS, :] = x3[owner[half, (it * 4 + j) * 16 + n]][0:ROWS]
            for m in range(3):
                to = pl.ds(pl.multiple_of(it * 384 + m * 128, 128), 128)
                xt[which, :, to] = xs[m * 128 : (m + 1) * 128, :].T.astype(jnp.bfloat16)

    for h in range(2):
        begin(upcopy(0, h))
        begin(downcopy(0, h))
        xsend(here, h)
    pl.semaphore_wait(far, 1)
    pl.semaphore_wait(back, 1)
    ends_send()
    zstep(1, 0)
    xsend(first[1], 0)
    xforward(here)
    zstep(1, 1)
    xsend(first[1], 1)
    inside = jnp.logical_not(edge)
    xsend_if(inside, second[1])
    zstep(2, 0)
    xsend(first[2], 0)
    xforward(first[1])
    zstep(2, 1)
    xsend(first[2], 1)
    finish(here)
    multiply(here)
    spread(here)
    begin(remote(sall.at[0, f], sr, q_s.at[0], q_r.at[0], cross))
    sent(sall.at[0, 0], q_s.at[0])
    ends_arrive()
    xforward(inner[2])
    finish(first[1])
    multiply(first[1])
    spread(first[1])
    xforward(inner[3])
    zstep(3, 0)
    zstep(3, 1)
    finish(inner[2])
    multiply(inner[2])
    finish(inner[3])
    multiply(inner[3])

    def build(fi, put):
        for n in range(16):
            put(slice(n * ROWS, (n + 1) * ROWS), y3[owner[g, fi * 16 + n]][0:ROWS])

    def cocopy(j):
        return remote(ycs.at[j], ycr.at[j], co_s, co_r.at[j], mate)

    allchips = [(0, 0)] + chips
    order_c = chips + [(0, 0)]
    for a, b in order_c:
        j = a * 4 + b

        def put(rows, v):
            pbuf[rows, :] = v

        def keep(rows, v):
            yown[j, rows, :] = v

        build(findex(a, b, 1), put)
        ycs[j] = pbuf[...].astype(jnp.bfloat16)
        begin(cocopy(j))
        build(findex(a, b, 0), keep)

    def ccopy(a, b):
        j = a * 4 + b
        return remote(cs.at[j], cr.at[j], c_s, c_r, fdev(a, b, 0))

    for a, b in order_c:
        j = a * 4 + b
        cocopy(j).wait_recv()
        total = yown[j] + ycr[j].astype(jnp.float32)
        if j:
            cs[j] = total.astype(jnp.bfloat16)
            begin(ccopy(a, b))
        else:
            pbuf[...] = total

    share(sall, 0, 0)
    sent(ycs, co_s)
    sent(cs.at[1:8], c_s)
    spread(inner[2])
    spread(inner[3])
    arrange(0, g, 0, 4)
    for k in outer[:2]:
        xsend(k, 0)
        xsend(k, 1)
    for h in range(2):
        zstep(4, h)

    got(cr.at[1:8], c_r)
    total = pbuf[...]
    for j in range(1, 8):
        total = total + cr[j].astype(jnp.float32)
    pbuf[...] = total

    target = sall[0, f].astype(jnp.float32)
    ones = jnp.ones((8, BS), jnp.float32)
    dims = (((1,), (1,)), ((), ()))
    sq = lax.dot_general(ones, total * total, dims, precision=HIGH, preferred_element_type=jnp.float32)
    sp = lax.dot_general(ones, total * target, dims, precision=HIGH, preferred_element_type=jnp.float32)
    which = lax.broadcasted_iota(jnp.int32, (2, BLOCK), 0)
    es[...] = jnp.zeros((2, 128), jnp.float32)
    es[:, 0:BLOCK] = jnp.where(which == 0, sq[0:2], sp[0:2])
    for m in range(1, 4):
        begin(remote(es, ex.at[m], e_s.at[0], e_r.at[0], dev(x=flip(x, m))))
    sent(ex.at[1:4], e_s.at[0])
    pall[0, f] = total.astype(jnp.bfloat16)
    begin(remote(pall.at[0, f], pr, q_s.at[1], q_r.at[1], cross))
    sent(pall.at[0, 0], q_s.at[1])
    xforward(outer[0])
    xforward(outer[1])
    got(ex.at[1:4], e_r.at[0])
    er[here] = es[...] + ex[1] + ex[2] + ex[3]
    for m in (4, 3, 5, 2, 6, 1, 7):
        begin(remote(er.at[here], er.at[here], e_s.at[1], e_r.at[1], zdev(2 * m)))
    sent(er.at[0:7], e_s.at[1])
    share(pall, 0, 1)
    for k in outer[2:]:
        xsend(k, 0)
        xsend(k, 1)
    for k in outer[:2]:
        finish(k)
        spread(k)
    relay(sall, 0, 0)
    got(sr, q_r.at[0])
    for k in outer[2:]:
        xforward(k)
    got(pr, q_r.at[1])

    got(er.at[0:7], e_r.at[1])
    sums = []
    for base in (g * 4, (1 - g) * 4):
        sums.append(er[base] + er[base + 1] + er[base + 2] + er[base + 3])
    factors = []
    for v in sums:
        sq, sp = v[0:1], v[1:2]
        root = jnp.sqrt(sq / DS + EPS)
        inner_mean = (sq / (root * root) - sp / root) / DS
        factors.append(((1.0 - inner_mean) / (root * root), 1.0 / root))
    sc[f] = jnp.concatenate(factors[0], axis=0)
    for a, b, e in fpeers:
        begin(remote(sc.at[f], sc.at[f], k_s, k_r, fdev(a, b, e)))
    sent(sc.at[0:15], k_s)

    def column(v):
        return jnp.broadcast_to(v, (128, 128)).T[0:BLOCK]

    def slope(state, tile, one, two):
        return (state.astype(jnp.float32) * one - tile.astype(jnp.float32) * two).astype(jnp.bfloat16)

    halves = [slice(m * 128, (m + 1) * 128) for m in range(2)]
    one, two = column(factors[1][0]), column(factors[1][1])
    for lanes in halves:
        dall[1, f, :, lanes] = slope(pr[:, lanes], sr[:, lanes], one, two)
    share(dall, 1, 2)
    relay(pall, 0, 1)
    for k in outer[2:]:
        finish(k)
        spread(k)
    arrange(1, 1 - g, 0, 4)
    def z_sent():
        block = lambda n: xg.at[0:n, 0]
        pl.when(edge)(remote(block(7), block(7), z_s, z_s, mate).wait_send)
        pl.when(edge)(remote(block(1), block(1), end_s, end_s, mate).wait_send)
        pl.when(inside)(remote(block(6), block(6), z_s, z_s, mate).wait_send)

    pending.append(z_sent)
    sent(xg.at[0:6], x_s)
    two = column(factors[0][1])
    for lanes in halves:
        gstud[:, lanes] = (target[:, lanes] - pbuf[:, lanes] * two).astype(jnp.bfloat16)
    settle(sall, 0, 0)
    settle(pall, 0, 1)
    got(sc.at[0:15], k_r)

    @pl.loop(0, 16)
    def _(n):
        rows = sc[n]
        one, two = column(rows[0:1]), column(rows[1:2])
        for lanes in halves:
            dall[0, n, :, lanes] = slope(pall[0, n, :, lanes], sall[0, n, :, lanes], one, two)

    relay(dall, 1, 2)
    part = jnp.dot(xt[0], dall[0].reshape(16 * BLOCK, BS), preferred_element_type=jnp.float32)
    settle(dall, 1, 2)
    part = part + jnp.dot(xt[1], dall[1].reshape(16 * BLOCK, BS), preferred_element_type=jnp.float32)
    gproj[...] = (part * SCALE).astype(jnp.bfloat16)
    for wait in pending:
        wait()


def shards(teacher, owner, proj_tiles, student_tiles):
    bf, f32 = jnp.bfloat16, jnp.float32
    vm, sem = pltpu.VMEM, pltpu.SemaphoreType.DMA
    one, pair = vm((1, 16, BLOCK, BS), bf), vm((2, 16, BLOCK, BS), bf)
    tile = vm((BLOCK, BS), bf)
    scratch = [
        vm((ROWS, 8192), bf), pltpu.SMEM((2, 256), jnp.int32), vm((BT, BS), bf), one,
        vm((16, ROWS, BT), bf), vm((BLOCK, BT), f32), vm((8, 4, BLOCK, BT), bf),
        vm((256, 8, BS), f32), vm((256, 8, BT), f32), vm((384, BT), f32), vm((2, BT, 1536), bf),
        vm((8, BLOCK, BS), bf), vm((8, BLOCK, BS), bf), vm((8, BLOCK, BS), f32),
        vm((8, BLOCK, BS), bf), vm((8, BLOCK, BS), bf), vm((BLOCK, BS), f32),
        one, tile, tile, vm((2, 128), f32), vm((4, 2, 128), f32), vm((8, 2, 128), f32), vm((16, 2, 128), f32), pair,
        sem((4,)), sem, sem, sem, sem, sem((8,)), sem((8,)), sem, sem((8,)), sem((8,)), sem((8,)),
        sem, sem((8,)), sem, sem, sem((2,)), sem((2,)),
        sem((2,)), sem((2,)), sem((3,)), sem((21,)), sem((3,)), sem, sem,
        pltpu.SemaphoreType.REGULAR, pltpu.SemaphoreType.REGULAR,
    ]
    whole = pl.BlockSpec(memory_space=pltpu.VMEM)
    anywhere = pl.BlockSpec(memory_space=pltpu.HBM)
    return pl.pallas_call(
        kernel,
        name="distill",
        out_shape=(jax.ShapeDtypeStruct((BT, BS), bf), jax.ShapeDtypeStruct((BLOCK, BS), bf)),
        in_specs=[anywhere] * 4,
        out_specs=(whole, whole),
        scratch_shapes=scratch,
        compiler_params=pltpu.CompilerParams(
            collective_id=0, has_side_effects=True, vmem_limit_bytes=36 * 2**20
        ),
    )(*(pltpu.with_memory_space_constraint(v, pltpu.HBM) for v in (teacher, owner, proj_tiles, student_tiles)))


def solution(mesh):
    placed = (P(("group", "dev"), None), P(), P("dev", None), P(("group", "dev"), None))
    return jax.shard_map(
        shards,
        mesh=mesh,
        in_specs=placed,
        out_specs=(P("dev", None), P(("group", "dev"), None)),
        check_vma=False,
    )
```

```python
import math

import jax
import jax.numpy as jnp
from jax import lax
from jax.experimental import pallas as pl
from jax.experimental.pallas import tpu as pltpu
from jax.sharding import PartitionSpec as P

MESH = pl.DeviceIdType.MESH
DS = 4096
EPS = 1e-06
HIGH = lax.Precision.HIGHEST
ROWS = 6
BLOCK = 96
HALF = BLOCK // 2
BT = 512
BS = 256
SCALE = 1.0 / math.sqrt(3072)


def flip(v, m):
    if m == 0:
        return v
    if m == 1:
        return v + 1 - 2 * (v % 2)
    if m == 2:
        return v + 2 - 4 * (v // 2)
    return 3 - v


def flip1(v, m):
    return 1 - v if m else v


def remote(src, dst, ss, rs, dev):
    return pltpu.make_async_remote_copy(
        src_ref=src, dst_ref=dst, send_sem=ss, recv_sem=rs, device_id=dev, device_id_type=MESH
    )


def kernel(
    teacher_in, owner_in, proj_in, student_in,
    gproj, gstud,
    teacher, owner, proj, sall,
    arecv, xa, xg, y3, x3, xs, xt, ycs, ycr, yown, cs, cr, pbuf, pall, pr, sr, es, ex, er, sc, dall,
    in_s, a_s, a_r, z_s, end_s, zu_r, zd_r, x_s, p_r, m_r, f_r, co_s, co_r, c_s, c_r, q_s, q_r,
    e_s, e_r, sh_s, sh_r, mate_r, k_s, k_r, far, back,
):
    g = lax.axis_index("group")
    d = lax.axis_index("dev")
    x, zl, y, c = d // 64, (d // 8) % 8, (d // 2) % 4, d % 2
    zk, z0 = zl // 2, zl % 2
    zz = g * 8 + zl

    def dev(x=x, zk=zk, z0=z0, y=y, c=c, g=g):
        return (g, ((x * 8 + zk * 2 + z0) * 4 + y) * 2 + c)

    def zdev(step):
        to = (zz + step) % 16
        return (to // 8, ((x * 8 + to % 8) * 4 + y) * 2 + c)

    f = z0 * 8 + y * 2 + c
    chips = [(a, b) for a in range(2) for b in range(4) if (a, b) != (0, 0)]
    fpeers = [(a, b, e) for a in range(2) for b in range(4) for e in range(2) if (a, b, e) != (0, 0, 0)]

    def fdev(a, b, e):
        return dev(z0=flip1(z0, a), y=flip(y, b), c=flip1(c, e))

    def findex(a, b, e):
        return flip1(z0, a) * 8 + flip(y, b) * 2 + flip1(c, e)

    xup, xdown = dev(x=(x + 1) % 4), dev(x=(x + 3) % 4)
    zup, zdown = zdev(2), zdev(14)
    here = g * 4 + zk
    mate, cross = dev(c=1 - c), dev(g=1 - g)
    left, right, opposite = (x + 3) % 4, (x + 1) % 4, (x + 2) % 4

    pending = []

    def begin(cp):
        cp.start()
        return cp

    def sent(ref, sem):
        pending.append(remote(ref, ref, sem, sem, mate).wait_send)

    def got(ref, sem):
        remote(ref, ref, sem, sem, mate).wait_recv()

    loads = [
        pltpu.make_async_copy(a, b, in_s.at[n])
        for n, (a, b) in enumerate(
            [(teacher_in, teacher), (owner_in, owner), (proj_in, proj), (student_in, sall.at[0, f])]
        )
    ]
    for cp in loads:
        cp.start()
    bar = pltpu.get_barrier_semaphore()

    def greet(to):
        pl.semaphore_signal(bar, inc=1, device_id=to, device_id_type=MESH)

    for step in (2, 14, 4, 12):
        greet(zdev(step))
    for a, b, e in fpeers:
        greet(fdev(a, b, e))
    greet(xup)
    greet(xdown)
    loads[0].wait()

    edge = (zk == 0) | (zk == 3)
    end = zdev(jnp.where(zk == 0, 6, 10))
    pl.semaphore_wait(bar, 21)
    pl.semaphore_signal(far, inc=1, device_id=zdev(4), device_id_type=MESH)
    pl.semaphore_signal(back, inc=1, device_id=zdev(12), device_id_type=MESH)

    for a, b, e in fpeers:
        to = findex(a, b, e)
        piece = teacher.at[:, pl.ds(pl.multiple_of(to * BT, BT), BT)]
        begin(remote(piece, arecv.at[f], a_s, a_r, fdev(a, b, e)))
    sent(arecv.at[0:15], a_s)
    arecv[f] = teacher[:, pl.ds(pl.multiple_of(f * BT, BT), BT)]

    def share(buf, s, n):
        for m, (a, b) in enumerate(chips):
            begin(remote(buf.at[s, f], buf.at[s, f], sh_s.at[n], sh_r.at[n * 7 + m], fdev(a, b, 0)))
        begin(remote(buf.at[s, f], buf.at[s, f], sh_s.at[n], mate_r.at[n], mate))
        sent(buf.at[s, 0:15], sh_s.at[n])

    def relay(buf, s, n):
        for m, (a, b) in enumerate(chips):
            block = buf.at[s, findex(a, b, 0)]
            got(block, sh_r.at[n * 7 + m])
            begin(remote(block, block, sh_s.at[n], mate_r.at[n], mate))

    def settle(buf, s, n):
        got(buf.at[s, 0:8], mate_r.at[n])

    for cp in loads[1:]:
        cp.wait()
    got(arecv.at[0:15], a_r)
    for n in range(16):
        xa[n * ROWS : (n + 1) * ROWS, :] = arecv[n].astype(jnp.float32)
    xg[here, x] = xa[...].astype(jnp.bfloat16)

    def view(k, at, h):
        return xg.at[k, at, pl.ds(h * HALF, HALF)]

    def below(s):
        return (here + 8 - s) % 8

    def above(s):
        return (here + s) % 8

    def upcopy(s, h):
        v = view(below(s), x, h)
        return remote(v, v, z_s, zu_r.at[s * 2 + h], zup)

    def downcopy(s, h):
        v = view(above(s), x, h)
        return remote(v, v, z_s, zd_r.at[s * 2 + h], zdown)

    def pcopy(k, at, h):
        v = view(k, at, h)
        return remote(v, v, x_s, f_r.at[k] if h else p_r.at[k], xup)

    def mcopy(k, at, h):
        v = view(k, at, h)
        return remote(v, v, x_s, m_r.at[k] if h else f_r.at[k], xdown)

    def hcopy(k, at, h):
        v = view(k, at, h)
        return remote(v, v, x_s, f_r.at[k], xdown if h else xup)

    def xforward(k):
        pcopy(k, left, 0).wait_recv()
        begin(hcopy(k, left, 0))
        mcopy(k, right, 1).wait_recv()
        begin(hcopy(k, right, 1))

    def finish(k):
        got(xg.at[k, 0:2], f_r.at[k])

    def xsend(k, h):
        begin(pcopy(k, x, h))
        begin(mcopy(k, x, h))

    def xsend_if(cond, k):
        @pl.when(cond)
        def _():
            xsend(k, 0)
            xsend(k, 1)

    def zstep(s, h):
        if s < 4 or h == 0:
            if s == 3:
                pl.when(zk != 3)(lambda: got(view(below(s), x, h), zu_r.at[4 + h]))
            else:
                got(view(below(s), x, h), zu_r.at[(s - 1) * 2 + h])
            if s == 2:
                pl.when(zk != 2)(upcopy(s, h).start)
            elif s < 2 or (s == 3 and h == 0):
                begin(upcopy(s, h))
        if s < 4 or h == 1:
            if s == 3:
                pl.when(zk != 0)(lambda: got(view(above(s), x, h), zd_r.at[4 + h]))
            else:
                got(view(above(s), x, h), zd_r.at[(s - 1) * 2 + h])
            if s == 2:
                pl.when(zk != 1)(downcopy(s, h).start)
            elif s < 2 or (s == 3 and h == 1):
                begin(downcopy(s, h))

    def ends_send():
        for h in range(2):
            v = view(here, x, h)
            pl.when(zk == 0)(remote(v, v, end_s, zu_r.at[4 + h], end).start)
            pl.when(zk == 3)(remote(v, v, end_s, zd_r.at[4 + h], end).start)

    def ends_arrive():
        for h in range(2):

            @pl.when(zk == 3)
            def _():
                got(view(below(3), x, h), zu_r.at[4 + h])
                xsend(below(3), h)

            @pl.when(zk == 0)
            def _():
                got(view(above(3), x, h), zd_r.at[4 + h])
                xsend(above(3), h)

    first, second = [here], [here]
    for s in range(1, 4):
        up_first = zk + s <= 3
        first.append(jnp.where(up_first, above(s), below(s)))
        second.append(jnp.where(up_first, below(s), above(s)))
    far_block = above(4)
    inner = [here, first[1], jnp.where(edge, first[2], second[1]), jnp.where(edge, first[3], first[2])]
    outer = [jnp.where(edge, second[1], second[2]), jnp.where(edge, second[2], first[3]), second[3], far_block]

    def multiply(k):
        part = jnp.dot(
            xg[k].reshape(4 * BLOCK, BT), proj[...], preferred_element_type=jnp.float32
        )
        for i in range(4):
            for n in range(16):
                r = (i * 16 + n) * ROWS
                y3[(i * 4 + k % 4) * 16 + n, 0:ROWS, :] = part[r : r + ROWS, :]

    def spread(k):
        @pl.loop(0, 4)
        def _(i):
            block = xg[k, i].astype(jnp.float32)
            for n in range(16):
                x3[(i * 4 + k % 4) * 16 + n, 0:ROWS, :] = block[n * ROWS : (n + 1) * ROWS, :]

    def arrange(which, half, first, last):
        @pl.loop(first, last)
        def _(it):
            for j in range(4):
                for n in range(16):
                    r = (j * 16 + n) * ROWS
                    xs[r : r + ROWS, :] = x3[owner[half, (it * 4 + j) * 16 + n]][0:ROWS]
            for m in range(3):
                to = pl.ds(pl.multiple_of(it * 384 + m * 128, 128), 128)
                xt[which, :, to] = xs[m * 128 : (m + 1) * 128, :].T.astype(jnp.bfloat16)

    for h in range(2):
        begin(upcopy(0, h))
        begin(downcopy(0, h))
        xsend(here, h)
    pl.semaphore_wait(far, 1)
    pl.semaphore_wait(back, 1)
    ends_send()
    zstep(1, 0)
    xsend(first[1], 0)
    xforward(here)
    zstep(1, 1)
    xsend(first[1], 1)
    inside = jnp.logical_not(edge)
    xsend_if(inside, second[1])
    zstep(2, 0)
    xsend(first[2], 0)
    xforward(first[1])
    zstep(2, 1)
    xsend(first[2], 1)
    finish(here)
    multiply(here)
    spread(here)
    begin(remote(sall.at[0, f], sr, q_s.at[0], q_r.at[0], cross))
    sent(sall.at[0, 0], q_s.at[0])
    ends_arrive()
    xforward(inner[2])
    finish(first[1])
    multiply(first[1])
    spread(first[1])
    xforward(inner[3])
    zstep(3, 0)
    zstep(3, 1)
    finish(inner[2])
    multiply(inner[2])
    finish(inner[3])
    multiply(inner[3])

    def build(fi, put):
        for n in range(16):
            put(slice(n * ROWS, (n + 1) * ROWS), y3[owner[g, fi * 16 + n]][0:ROWS])

    def cocopy(j):
        return remote(ycs.at[j], ycr.at[j], co_s, co_r.at[j], mate)

    allchips = [(0, 0)] + chips
    order_c = chips + [(0, 0)]
    for a, b in order_c:
        j = a * 4 + b

        def put(rows, v):
            pbuf[rows, :] = v

        def keep(rows, v):
            yown[j, rows, :] = v

        build(findex(a, b, 1), put)
        ycs[j] = pbuf[...].astype(jnp.bfloat16)
        begin(cocopy(j))
        build(findex(a, b, 0), keep)

    def ccopy(a, b):
        j = a * 4 + b
        return remote(cs.at[j], cr.at[j], c_s, c_r, fdev(a, b, 0))

    for a, b in order_c:
        j = a * 4 + b
        cocopy(j).wait_recv()
        total = yown[j] + ycr[j].astype(jnp.float32)
        if j:
            cs[j] = total.astype(jnp.bfloat16)
            begin(ccopy(a, b))
        else:
            pbuf[...] = total

    share(sall, 0, 0)
    sent(ycs, co_s)
    sent(cs.at[1:8], c_s)
    spread(inner[2])
    spread(inner[3])
    arrange(0, g, 0, 4)
    for k in outer[:2]:
        xsend(k, 0)
        xsend(k, 1)
    for h in range(2):
        zstep(4, h)

    got(cr.at[1:8], c_r)
    total = pbuf[...]
    for j in range(1, 8):
        total = total + cr[j].astype(jnp.float32)
    pbuf[...] = total

    target = sall[0, f].astype(jnp.float32)
    ones = jnp.ones((8, BS), jnp.float32)
    dims = (((1,), (1,)), ((), ()))
    sq = lax.dot_general(ones, total * total, dims, precision=HIGH, preferred_element_type=jnp.float32)
    sp = lax.dot_general(ones, total * target, dims, precision=HIGH, preferred_element_type=jnp.float32)
    which = lax.broadcasted_iota(jnp.int32, (2, BLOCK), 0)
    es[...] = jnp.zeros((2, 128), jnp.float32)
    es[:, 0:BLOCK] = jnp.where(which == 0, sq[0:2], sp[0:2])
    for m in range(1, 4):
        begin(remote(es, ex.at[m], e_s.at[0], e_r.at[0], dev(x=flip(x, m))))
    sent(ex.at[1:4], e_s.at[0])
    pall[0, f] = total.astype(jnp.bfloat16)
    begin(remote(pall.at[0, f], pr, q_s.at[1], q_r.at[1], cross))
    sent(pall.at[0, 0], q_s.at[1])
    xforward(outer[0])
    xforward(outer[1])
    got(ex.at[1:4], e_r.at[0])
    er[here] = es[...] + ex[1] + ex[2] + ex[3]
    for m in (4, 3, 5, 2, 6, 1, 7):
        begin(remote(er.at[here], er.at[here], e_s.at[1], e_r.at[1], zdev(2 * m)))
    sent(er.at[0:7], e_s.at[1])
    share(pall, 0, 1)
    for k in outer[2:]:
        xsend(k, 0)
        xsend(k, 1)
    for k in outer[:2]:
        finish(k)
        spread(k)
    relay(sall, 0, 0)
    got(sr, q_r.at[0])
    for k in outer[2:]:
        xforward(k)
    got(pr, q_r.at[1])

    got(er.at[0:7], e_r.at[1])
    sums = []
    for base in (g * 4, (1 - g) * 4):
        sums.append(er[base] + er[base + 1] + er[base + 2] + er[base + 3])
    factors = []
    for v in sums:
        sq, sp = v[0:1], v[1:2]
        root = jnp.sqrt(sq / DS + EPS)
        inner_mean = (sq / (root * root) - sp / root) / DS
        factors.append(((1.0 - inner_mean) / (root * root), 1.0 / root))
    sc[f] = jnp.concatenate(factors[0], axis=0)
    for a, b, e in fpeers:
        begin(remote(sc.at[f], sc.at[f], k_s, k_r, fdev(a, b, e)))
    sent(sc.at[0:15], k_s)

    def column(v):
        return jnp.broadcast_to(v, (128, 128)).T[0:BLOCK]

    def slope(state, tile, one, two):
        return (state.astype(jnp.float32) * one - tile.astype(jnp.float32) * two).astype(jnp.bfloat16)

    halves = [slice(m * 128, (m + 1) * 128) for m in range(2)]
    one, two = column(factors[1][0]), column(factors[1][1])
    for lanes in halves:
        dall[1, f, :, lanes] = slope(pr[:, lanes], sr[:, lanes], one, two)
    share(dall, 1, 2)
    relay(pall, 0, 1)
    for k in outer[2:]:
        finish(k)
        spread(k)
    arrange(1, 1 - g, 0, 4)
    def z_sent():
        block = lambda n: xg.at[0:n, 0]
        pl.when(edge)(remote(block(7), block(7), z_s, z_s, mate).wait_send)
        pl.when(edge)(remote(block(1), block(1), end_s, end_s, mate).wait_send)
        pl.when(inside)(remote(block(6), block(6), z_s, z_s, mate).wait_send)

    pending.append(z_sent)
    sent(xg.at[0:6], x_s)
    two = column(factors[0][1])
    for lanes in halves:
        gstud[:, lanes] = (target[:, lanes] - pbuf[:, lanes] * two).astype(jnp.bfloat16)
    settle(sall, 0, 0)
    settle(pall, 0, 1)
    got(sc.at[0:15], k_r)

    @pl.loop(0, 16, unroll=4)
    def _(n):
        rows = sc[n]
        one, two = column(rows[0:1]), column(rows[1:2])
        for lanes in halves:
            dall[0, n, :, lanes] = slope(pall[0, n, :, lanes], sall[0, n, :, lanes], one, two)

    relay(dall, 1, 2)
    part = jnp.dot(xt[0], dall[0].reshape(16 * BLOCK, BS), preferred_element_type=jnp.float32)
    settle(dall, 1, 2)
    part = part + jnp.dot(xt[1], dall[1].reshape(16 * BLOCK, BS), preferred_element_type=jnp.float32)
    gproj[...] = (part * SCALE).astype(jnp.bfloat16)
    for wait in pending:
        wait()


def shards(teacher, owner, proj_tiles, student_tiles):
    bf, f32 = jnp.bfloat16, jnp.float32
    vm, sem = pltpu.VMEM, pltpu.SemaphoreType.DMA
    one, pair = vm((1, 16, BLOCK, BS), bf), vm((2, 16, BLOCK, BS), bf)
    tile = vm((BLOCK, BS), bf)
    scratch = [
        vm((ROWS, 8192), bf), pltpu.SMEM((2, 256), jnp.int32), vm((BT, BS), bf), one,
        vm((16, ROWS, BT), bf), vm((BLOCK, BT), f32), vm((8, 4, BLOCK, BT), bf),
        vm((256, 8, BS), f32), vm((256, 8, BT), f32), vm((384, BT), f32), vm((2, BT, 1536), bf),
        vm((8, BLOCK, BS), bf), vm((8, BLOCK, BS), bf), vm((8, BLOCK, BS), f32),
        vm((8, BLOCK, BS), bf), vm((8, BLOCK, BS), bf), vm((BLOCK, BS), f32),
        one, tile, tile, vm((2, 128), f32), vm((4, 2, 128), f32), vm((8, 2, 128), f32), vm((16, 2, 128), f32), pair,
        sem((4,)), sem, sem, sem, sem, sem((8,)), sem((8,)), sem, sem((8,)), sem((8,)), sem((8,)),
        sem, sem((8,)), sem, sem, sem((2,)), sem((2,)),
        sem((2,)), sem((2,)), sem((3,)), sem((21,)), sem((3,)), sem, sem,
        pltpu.SemaphoreType.REGULAR, pltpu.SemaphoreType.REGULAR,
    ]
    whole = pl.BlockSpec(memory_space=pltpu.VMEM)
    anywhere = pl.BlockSpec(memory_space=pltpu.HBM)
    return pl.pallas_call(
        kernel,
        name="distill",
        out_shape=(jax.ShapeDtypeStruct((BT, BS), bf), jax.ShapeDtypeStruct((BLOCK, BS), bf)),
        in_specs=[anywhere] * 4,
        out_specs=(whole, whole),
        scratch_shapes=scratch,
        compiler_params=pltpu.CompilerParams(
            collective_id=0, has_side_effects=True, vmem_limit_bytes=36 * 2**20
        ),
    )(*(pltpu.with_memory_space_constraint(v, pltpu.HBM) for v in (teacher, owner, proj_tiles, student_tiles)))


def solution(mesh):
    placed = (P(("group", "dev"), None), P(), P("dev", None), P(("group", "dev"), None))
    return jax.shard_map(
        shards,
        mesh=mesh,
        in_specs=placed,
        out_specs=(P("dev", None), P(("group", "dev"), None)),
        check_vma=False,
    )
```
